128 devices in a mesh: node: 8 (over y_lo, z), bond: 16 (over y_hi, x, core).
Axes of the slice: x: 4, y: 4 (y_hi: 2, y_lo: 2; y = y_hi * 2 + y_lo), z: 4, core: 2. Of those that a mesh axis runs over, the one named last changes fastest.
Arguments:
- bottom_nodes: float32 [8, 128, 128, 128], P('node', 'bond'), may hold values from -0.046875 to 0.046875
- upper_nodes: float32 [8, 128, 128, 128], P(None, 'bond', 'node'), may hold values from -0.046875 to 0.046875
- leaf_up: float32 [8, 3, 2, 128, 128], P('node'), may hold values from -2 to 3
- outside_env: float32 [3, 128, 128], replicated, may hold values from -2 to 3
- top_env: float32 [3, 128, 128], replicated, may hold values from -2 to 3
Outputs:
- leaf_down: float32 [8, 3, 2, 128, 128], P('node', None, None, 'bond')
- subtree_env: float32 [3, 128, 128], replicated
The draws below stay inside these ranges and needn't reach their ends.
All inputs are finite; a program needn't handle non-finite values.
Results may differ from the reference program's by a relative error of at most 0.0001.
Values sent between devices are 32-bit elements; how exact they have to be, the bound alone decides.
No kernel may reach another device: no remote copies, remote signals or barrier semaphores. Data moves between devices by JAX's collectives and lax.ppermute only.
A program may use at most 128 MiB of HBM per device.

```python
import math
import jax
import jax.numpy as jnp
from jax import lax

D = 128
OPS = 3
NODES = 8


def env_matrix(key, shape):
    identity = jnp.eye(D, dtype=jnp.float32)
    spread = jnp.clip(jax.random.normal(key, shape, jnp.float32), -6.0, 6.0) * (3.0 / math.sqrt(D))
    return identity + spread


def draw_leaf_up(key, part):
    return env_matrix(jax.random.fold_in(key, 11), (NODES, OPS, 2, D, D))


def draw_outside_env(key, part):
    return env_matrix(jax.random.fold_in(key, 23), (OPS, D, D))


def draw_top_env(key, part):
    return env_matrix(jax.random.fold_in(key, 37), (OPS, D, D))


def steps_of(stream_key, shape, pieces, low, high):
    def one(axis_at, blocks):
        heights = jax.random.uniform(jax.random.fold_in(jax.random.fold_in(stream_key, 6), axis_at), (blocks,), jnp.float32, low / len(pieces), high / len(pieces))
        return jnp.repeat(jnp.exp(heights), shape[axis_at] // blocks).reshape((-1,) + (1,) * (len(shape) - axis_at - 1))

    loudness = one(*pieces[0])
    for cut in pieces[1:]:
        loudness = loudness * one(*cut)
    return loudness


def normal_values(stream_key, extent, deviation, limit, cuts=(), kind=jnp.bfloat16):
    gain = steps_of(stream_key, extent, cuts, -0.22, 0.18) if cuts else 1.0
    entries = jax.random.normal(stream_key, extent, jnp.float32) * deviation * gain
    return jnp.minimum(jnp.maximum(entries, -limit), limit).astype(kind)


def setup_inputs(seed: int = 0) -> dict:
    splits = jax.random.split(jax.random.key(seed), 6)
    return {
        "bottom_nodes": normal_values(splits[0], (NODES, D, D, D), (D * D) ** -0.5, 0.046875, ((0, 8), (1, 16)), jnp.float32),
        "upper_nodes": normal_values(splits[1], (NODES, D, D, D), (D * D) ** -0.5, 0.046875, ((1, 16), (2, 8)), jnp.float32),
        "leaf_up": draw_leaf_up(jax.random.fold_in(splits[5], 71), 0),
        "outside_env": draw_outside_env(jax.random.fold_in(splits[5], 71), 0),
        "top_env": draw_top_env(jax.random.fold_in(splits[5], 71), 0),
    }


highest = lax.Precision.HIGHEST


def grow_env(tensor, left_env, right_env):
    middle = jnp.einsum('kac,pcd->kpad', left_env, tensor, precision=highest)
    product = jnp.einsum('kpad,kbd->kpab', middle, right_env, precision=highest)
    return jnp.einsum('pab,kqab->kpq', tensor, product, precision=highest)


def split_env(tensor, above, left_env, right_env):
    worked = jnp.einsum('kpq,qcd->kpcd', above, tensor, precision=highest)
    first = jnp.einsum('kpcd,kbd->kpcb', worked, right_env, precision=highest)
    first_env = jnp.einsum('pab,kpcb->kac', tensor, first, precision=highest)
    second = jnp.einsum('kac,kpcd->kpad', left_env, worked, precision=highest)
    second_env = jnp.einsum('pab,kpad->kbd', tensor, second, precision=highest)
    return first_env, second_env


def reference(bottom_nodes, upper_nodes, leaf_up, outside_env, top_env):
    nodes = NODES
    ups = [None] * (2 * nodes)
    for index in range(nodes):
        ups[nodes + index] = grow_env(bottom_nodes[index], leaf_up[index, :, 0], leaf_up[index, :, 1])
    for slot in range(nodes - 1, 0, -1):
        ups[slot] = grow_env(upper_nodes[slot], ups[2 * slot], ups[2 * slot + 1])
    downs = [None] * (2 * nodes)
    downs[1] = split_env(upper_nodes[0], top_env, ups[1], outside_env)[0]
    for slot in range(1, nodes):
        first_env, second_env = split_env(upper_nodes[slot], downs[slot], ups[2 * slot], ups[2 * slot + 1])
        downs[2 * slot] = first_env
        downs[2 * slot + 1] = second_env
    leaves = []
    for index in range(nodes):
        first_env, second_env = split_env(bottom_nodes[index], downs[nodes + index], leaf_up[index, :, 0], leaf_up[index, :, 1])
        leaves.append(jnp.stack([first_env, second_env], 1))
    return jnp.stack(leaves), ups[1]
```

```python
import jax
import jax.numpy as jnp
from jax import lax
from jax.sharding import Mesh, PartitionSpec as P

NODE = ("ylo", "zhi", "zlo")
BOND = ("yhi", "x", "core")
SLOT_OF = (4, 2, 5, 1, 6, 3, 7, 0)


def ein(spec, a, b):
    return jnp.einsum(spec, a, b, precision=lax.Precision.HIGHEST)


def after(x, other):
    return lax.optimization_barrier((x, other))[0]


def swap_cores(half, core, axis):
    other = lax.ppermute(half, "core", [(0, 1), (1, 0)])
    low = jnp.where(core == 0, half, other)
    high = jnp.where(core == 0, other, half)
    return jnp.concatenate([low, high], axis=axis)


def up_rows(tensor, rows, left_env, right_env):
    middle = ein("pab,ac->pcb", rows, left_env)
    product = ein("pcb,bd->pcd", middle, right_env)
    return ein("pcd,qcd->pq", product, tensor)


def halves(tensor, core, axis):
    size = tensor.shape[axis] // 2
    return lax.dynamic_slice_in_dim(tensor, core * size, size, axis=axis)


def local(bottom_nodes, upper_nodes, leaf_up, outside_env, top_env):
    group = lax.axis_index(NODE)
    bond = lax.axis_index(BOND)
    core = lax.axis_index("core")
    op = jnp.minimum(lax.axis_index("x"), 2)
    width = bottom_nodes.shape[2]
    rows = bottom_nodes.shape[1]
    parts = width // rows

    send = jnp.stack([upper_nodes[s] for s in SLOT_OF])
    got = lax.all_to_all(send, NODE, 0, 0, tiled=True)
    shard = jnp.moveaxis(got, 0, 1).reshape(rows, width, width)
    upper = lax.all_gather(shard, BOND, axis=0, tiled=True)

    mine = bottom_nodes[0]
    left_leaf = leaf_up[0, :, 0]
    right_leaf = leaf_up[0, :, 1]
    middle = ein("kac,pcd->kpad", left_leaf, after(mine, shard))
    product = ein("kpad,kbd->kpab", middle, right_leaf)
    both = jnp.concatenate([mine[None], product])
    both = jnp.moveaxis(both.reshape(4, rows, parts, rows, width), 2, 0)
    both = lax.all_to_all(both, BOND, 0, 0, tiled=True)
    both = jnp.moveaxis(both, 1, 0).reshape(4, width, rows, width)
    mine_a = both[0]
    gram = ein("pab,kqab->kpq", mine_a, both[1:])
    pieces = jnp.moveaxis(gram.reshape(3, parts, rows, width), 1, 0)
    pieces = lax.all_to_all(pieces, BOND, 0, 0, tiled=True)
    env = jnp.sum(pieces, axis=0)
    by_x = jnp.stack([env[0], env[1], env[2], env[2]])
    by_dest = jnp.broadcast_to(by_x[None, None, :, None], (2, 2, 4, 2, rows, width))
    by_dest = by_dest.reshape(2 * parts, rows, width)
    pair = lax.all_to_all(by_dest, ("zlo",) + BOND, 0, 0, tiled=True)
    left3, right3 = pair.reshape(2, width, width)

    def move(x, *pairs):
        return lax.ppermute(x, NODE, pairs)

    upper_rows = halves(upper, core, 0)
    up2 = up_rows(upper, upper_rows, left3, right3)
    ends = jnp.stack([move(up2, (0, 1), (4, 5)), move(up2, (2, 1), (6, 5))])
    left2, right2 = swap_cores(ends, core, 1)
    up1 = up_rows(upper, upper_rows, left2, right2)
    ends = jnp.stack([move(up1, (1, 3)), move(up1, (5, 3))])
    left1, right1 = swap_cores(ends, core, 1)

    upper_a = halves(upper, core, 1)
    upper_b = halves(upper, core, 2)

    def first_row(right_env):
        return ein("pab,bd->pad", upper_a, right_env)

    def second_row(left_env):
        return ein("pab,ac->pcb", upper_b, left_env)

    def worked_by(above):
        return ein("pq,qcd->pcd", above, upper)

    def first_of(row, worked):
        return ein("pad,pcd->ac", row, worked)

    def second_of(row, worked):
        return ein("pcb,pcd->bd", row, worked)

    top = lax.dynamic_index_in_dim(top_env, op, 0, keepdims=False)
    outside = lax.dynamic_index_in_dim(outside_env, op, 0, keepdims=False)
    crown = first_of(first_row(outside), worked_by(top))
    above = swap_cores(move(crown, (7, 3)), core, 0)
    worked = worked_by(above)
    first = first_of(first_row(right1), worked)
    second = second_of(second_row(left1), worked)
    root = up_rows(upper, upper_rows, left1, right1)
    above = swap_cores(move(first, (3, 1)) + move(second, (3, 5)), core, 0)
    worked = worked_by(above)
    first = first_of(first_row(right2), worked)
    second = second_of(second_row(left2), worked)
    above = move(first, (1, 0), (5, 4)) + move(second, (1, 2), (5, 6))
    above = swap_cores(above, core, 0)
    worked = worked_by(above)
    first = first_of(first_row(right3), worked)
    second = second_of(second_row(left3), worked)
    sent = move(second, (0, 1), (2, 3), (4, 5), (6, 7))
    last = jnp.where(group % 2 == 0, first, sent)

    root = jnp.where(group == 3, root, 0.0)
    root = root + move(root, (3, 7))
    root = root + move(root, (3, 1), (7, 5))
    root = root + move(root, (3, 2), (1, 0), (7, 6), (5, 4))
    ends = lax.all_gather(jnp.stack([last, root]), "x", axis=0, tiled=False)
    ends = swap_cores(ends[:3], core, 2)
    above = ends[:, 0]
    root_env = ends[:, 1]

    whole = lax.all_gather(after(mine, upper), BOND, axis=0, tiled=True)
    row = ein("pab,kbd->kpad", mine_a, right_leaf)
    grown = ein("kpq,kpad->kqad", above, row)
    first = ein("kqad,qcd->kac", grown, whole)
    turned = lax.dynamic_slice_in_dim(jnp.swapaxes(whole, 1, 2), bond * rows, rows, axis=1)
    row = ein("pba,kac->kbpc", turned, left_leaf)
    grown = ein("kpq,kbpc->kbqc", above, row)
    second = ein("kbqc,qcd->kbd", grown, whole)
    leaf_down = jnp.stack([first, second], 1)[None]
    return leaf_down, root_env


def solution(mesh):
    shape = (2, 2, 2, 2, 4, 2)
    fine = Mesh(mesh.devices.reshape(shape), NODE + BOND)
    placed = (
        P(NODE, BOND, None, None),
        P(None, BOND, NODE, None),
        P(NODE, None, None, None, None),
        P(),
        P(),
    )
    return jax.shard_map(
        local,
        mesh=fine,
        in_specs=placed,
        out_specs=(P(NODE, None, None, BOND, None), P()),
        check_vma=False,
    )
```

```python
import functools

import jax
import jax.numpy as jnp
from jax import lax
from jax.experimental import pallas as pl
from jax.experimental.pallas import tpu as pltpu
from jax.sharding import Mesh, PartitionSpec as P

BF = jnp.bfloat16
F32 = jnp.float32
CHUNKS = 8


def split(v):
    hi = v.astype(BF)
    return hi, (v - hi.astype(F32)).astype(BF)


def wide(v):
    return jnp.concatenate(split(v), axis=1)


def stacked(v):
    row = wide(v)
    return jnp.concatenate([row, row], axis=0)


def mm(a, b):
    return jnp.dot(a, b, preferred_element_type=F32)


def mm_t(a, b):
    return lax.dot_general(a, b, (((1,), (1,)), ((), ())), preferred_element_type=F32)


def fold(v):
    half = v.shape[1] // 2
    return v[:, :half] + v[:, half:]


def product(a_wide, b_stacked):
    return fold(mm(a_wide, b_stacked))


def pair_rows(one, two):
    h1, l1 = split(one)
    h2, l2 = split(two)
    return jnp.concatenate([jnp.concatenate([h1, h2], 1), jnp.concatenate([l1, l2], 1)], 0)


def quarters(acc):
    r = acc.shape[0] // 2
    c = acc.shape[1] // 2
    return (acc[:r, :c] + acc[r:, :c]) + (acc[:r, c:] + acc[r:, c:])


def aligned(i, n):
    return pl.multiple_of(i * n, n)


def fetch(src, dst, sems, count, first=0):
    size = dst.shape[0] // count

    def copy(i):
        at = lax.rem(first + i, count)
        there = pl.ds(aligned(at, size), size)
        return pltpu.make_async_copy(src.at[there], dst.at[there], sems.at[i])

    return copy


def up_kernel(D, H, place_ref, x_hbm, l_ref, r_ref, out_ref, x_ref, n_scr, sems):
    @pl.when(place_ref[2] == 0)
    def _():
        out_ref[...] = jnp.zeros_like(out_ref)

    @pl.when(place_ref[2] == 1)
    def _():
        count = 2 * CHUNKS
        copy = fetch(x_hbm, x_ref, sems, count, place_ref[0] * CHUNKS)
        for i in range(count):
            copy(i).start()
        start = place_ref[0] * H
        rr = stacked(r_ref[...])
        ll = wide(l_ref[...].T)
        per = H // CHUNKS

        def chunk(i, carry):
            copy(i).wait()
            for j in range(per):
                p = i * per + j
                t = product(wide(x_ref[pl.ds(aligned(start + p, D), D), :]), rr)
                n_scr[pl.ds(p, D, stride=H), :] = product(ll, stacked(t))
            return carry

        lax.fori_loop(0, CHUNKS, chunk, 0)
        for i in range(CHUNKS, count):
            copy(i).wait()

        def gram(i, acc):
            c = 2 * i
            lhs = pair_rows(n_scr[pl.ds(aligned(c, H), H), :], n_scr[pl.ds(aligned(c + 1, H), H), :])
            rhs = pair_rows(x_ref[pl.ds(c, D, stride=D), :], x_ref[pl.ds(c + 1, D, stride=D), :])
            return acc + mm_t(lhs, rhs)

        acc = lax.fori_loop(0, D // 2, gram, jnp.zeros((2 * H, 2 * D), F32), unroll=8)
        out_ref[...] = quarters(acc)


def side_kernel(D, H, place_ref, x_hbm, l_ref, r_ref, s_hbm, x_ref, s_ref, sems):
    @pl.when(place_ref[2] == 1)
    def _():
        copy = fetch(x_hbm, x_ref, sems, CHUNKS)
        for i in range(CHUNKS):
            copy(i).start()
        start = place_ref[0] * H
        per = D // CHUNKS

        @pl.when(place_ref[1] == 0)
        def _():
            rr = stacked(r_ref[...])

            def chunk(i, carry):
                copy(i).wait()
                for j in range(per):
                    p = i * per + j
                    x = x_ref[pl.ds(aligned(2 * p + place_ref[0], H), H), :]
                    s_ref[pl.ds(p, H, stride=D), :] = product(wide(x), rr)
                return carry

            lax.fori_loop(0, CHUNKS, chunk, 0)

        @pl.when(place_ref[1] == 1)
        def _():
            ll = wide(l_ref[...].T)
            half = jnp.where(place_ref[0] == 0, ll[:H], ll[H:])

            def chunk(i, carry):
                copy(i).wait()
                for j in range(per):
                    p = i * per + j
                    x = x_ref[pl.ds(aligned(p, D), D), :]
                    s_ref[pl.ds(p, H, stride=D), :] = product(half, stacked(x))
                return carry

            lax.fori_loop(0, CHUNKS, chunk, 0)

        done = pltpu.make_async_copy(s_ref, s_hbm, sems.at[0])
        done.start()
        done.wait()


def down_kernel(D, H, place_ref, x_hbm, s_hbm, e_ref, out_ref, x_ref, s_ref, n_scr, sems):
    out_ref[...] = jnp.zeros_like(out_ref)

    @pl.when(place_ref[2] == 1)
    def _():
        s_copy = fetch(s_hbm, s_ref, sems, CHUNKS)
        x_copy = fetch(x_hbm, x_ref, sems.at[pl.ds(CHUNKS, CHUNKS)], CHUNKS)
        for i in range(CHUNKS):
            s_copy(i).start()
        for i in range(CHUNKS):
            x_copy(i).start()
        start = place_ref[0] * H
        ee = wide(e_ref[...].T)
        per = H // CHUNKS

        def chunk(i, carry):
            s_copy(i).wait()
            for j in range(per):
                v = i * per + j
                t = s_ref[pl.ds(aligned(v, D), D), :]
                n_scr[pl.ds(v, D, stride=H), :] = product(ee, stacked(t))
            return carry

        lax.fori_loop(0, CHUNKS, chunk, 0)
        for i in range(CHUNKS):
            x_copy(i).wait()

        @pl.when(place_ref[1] == 0)
        def _():
            def gram(i, acc):
                q = 2 * i
                lhs = pair_rows(n_scr[pl.ds(aligned(q, H), H), :], n_scr[pl.ds(aligned(q + 1, H), H), :])
                rhs = pair_rows(x_ref[pl.ds(aligned(q, D), D), :], x_ref[pl.ds(aligned(q + 1, D), D), :])
                return acc + mm_t(lhs, rhs)

            acc = lax.fori_loop(0, D // 2, gram, jnp.zeros((2 * H, 2 * D), F32), unroll=8)
            out_ref[pl.ds(aligned(place_ref[0], H), H), :] = quarters(acc)

        @pl.when(place_ref[1] == 1)
        def _():
            def gram(i, acc):
                q = 4 * i
                v = n_scr[pl.ds(aligned(i, 4 * H), 4 * H), :].T
                lhs = jnp.concatenate(split(v), 0)
                x = [x_ref[pl.ds(pl.multiple_of((q + j) * D + start, H), H), :] for j in range(4)]
                return acc + mm(lhs, wide(jnp.concatenate(x, 0)))

            acc = lax.fori_loop(0, D // 4, gram, jnp.zeros((2 * D, 2 * D), F32), unroll=4)
            out_ref[...] = quarters(acc)


def leaf_side_kernel(D, W, K, at_ref, x_hbm, xa_ref, l_ref, r_ref, t_ref, u_ref, x_ref, b_scr, sems):
    copy = fetch(x_hbm, x_ref, sems, CHUNKS)
    for i in range(CHUNKS):
        copy(i).start()
    for k in range(K):
        rr = stacked(r_ref[k])
        for a in range(W):
            x = xa_ref[pl.ds(a, D, stride=W), :]
            t_ref[pl.ds((k * W + a) * D, D), :] = product(wide(x), rr)
    lane = lax.broadcasted_iota(jnp.int32, (W, D), 1)
    line = lax.broadcasted_iota(jnp.int32, (W, D), 0)
    pick = jnp.where(lane == line + at_ref[0] * W, 1.0, 0.0).astype(BF)
    per = D // CHUNKS

    def chunk(i, carry):
        copy(i).wait()
        for j in range(per):
            p = i * per + j
            x = x_ref[pl.ds(aligned(p, D), D), :]
            b_scr[pl.ds(p, W, stride=D), :] = fold(mm_t(pick, jnp.concatenate(split(x), 0)))
        return carry

    lax.fori_loop(0, CHUNKS, chunk, 0)
    for k in range(K):
        ll = stacked(l_ref[k])
        for b in range(W):
            u_ref[pl.ds((k * W + b) * D, D), :] = product(wide(b_scr[pl.ds(b * D, D), :]), ll)


def leaf_kernel(D, W, K, x_hbm, t_ref, u_ref, e_ref, out_ref, x_ref, n_scr, v_scr, sems):
    copy = fetch(x_hbm, x_ref, sems, CHUNKS)
    for i in range(CHUNKS):
        copy(i).start()
    R = K * W
    for k in range(K):
        ee = wide(e_ref[k].T)
        for w in range(W):
            r = k * W + w
            n_scr[pl.ds(r, D, stride=R), :] = product(ee, stacked(t_ref[pl.ds(r * D, D), :]))
            v_scr[pl.ds(r, D, stride=R), :] = product(ee, stacked(u_ref[pl.ds(r * D, D), :]))
    for i in range(CHUNKS):
        copy(i).wait()

    def gram(i, accs):
        q = 2 * i
        one, two = pl.ds(aligned(q, R), R), pl.ds(aligned(q + 1, R), R)
        h1, l1 = split(x_ref[pl.ds(aligned(q, D), D), :])
        h2, l2 = split(x_ref[pl.ds(aligned(q + 1, D), D), :])
        cat = jnp.concatenate
        by_last = cat([cat([h1, h2], 1), cat([l1, l2], 1)], 0)
        by_first = cat([cat([h1, l1], 1), cat([h2, l2], 1)], 0)
        first = mm_t(pair_rows(n_scr[one, :], n_scr[two, :]), by_last)
        second = mm(pair_rows(v_scr[one, :], v_scr[two, :]), by_first)
        return accs[0] + first, accs[1] + second

    zero = jnp.zeros((2 * R, 2 * D), F32)
    first, second = lax.fori_loop(0, D // 2, gram, (zero, zero), unroll=4)
    first = quarters(first)
    second = quarters(second)
    for k in range(K):
        out_ref[k, 0] = first[k * W : (k + 1) * W]
        out_ref[k, 1] = second[k * W : (k + 1) * W]


VMEM = pl.BlockSpec(memory_space=pltpu.VMEM)
SMEM = pl.BlockSpec(memory_space=pltpu.SMEM)
HBM = pl.BlockSpec(memory_space=pltpu.HBM)


def call(kernel, name, mib, units, out_shape, in_specs, out_specs, scratch):
    return pl.pallas_call(
        kernel,
        out_shape=out_shape,
        in_specs=in_specs,
        out_specs=out_specs,
        scratch_shapes=scratch,
        compiler_params=pltpu.CompilerParams(vmem_limit_bytes=mib << 20),
        cost_estimate=pl.CostEstimate(
            flops=int(units * 4.8e9), bytes_accessed=8 << 20, transcendentals=0
        ),
        name=name,
    )


def up_rows(place, tensor, left_env, right_env):
    D = left_env.shape[0]
    H = D // 2
    return call(
        functools.partial(up_kernel, D, H),
        "up",
        24,
        1,
        jax.ShapeDtypeStruct((H, D), F32),
        [SMEM, HBM, VMEM, VMEM],
        VMEM,
        [pltpu.VMEM((D * D, D), F32), pltpu.VMEM((D * H, D), F32), pltpu.SemaphoreType.DMA((2 * CHUNKS,))],
    )(place, tensor.reshape(D * D, D), left_env, right_env)


def side_part(place, tensor, left_env, right_env):
    D = left_env.shape[0]
    H = D // 2
    return call(
        functools.partial(side_kernel, D, H),
        "side",
        24,
        0.4,
        jax.ShapeDtypeStruct((D * H, D), F32),
        [SMEM, HBM, VMEM, VMEM],
        HBM,
        [pltpu.VMEM((D * D, D), F32), pltpu.VMEM((D * H, D), F32), pltpu.SemaphoreType.DMA((CHUNKS,))],
    )(place, tensor.reshape(D * D, D), left_env, right_env)


def down_part(place, tensor, side, above):
    D = above.shape[0]
    H = D // 2
    big = pltpu.VMEM((D * D, D), F32)
    half = pltpu.VMEM((D * H, D), F32)
    return call(
        functools.partial(down_kernel, D, H),
        "down",
        28,
        0.7,
        jax.ShapeDtypeStruct((D, D), F32),
        [SMEM, HBM, HBM, VMEM],
        VMEM,
        [big, half, half, pltpu.SemaphoreType.DMA((2 * CHUNKS,))],
    )(place, tensor.reshape(D * D, D), side, above)


def leaf_sides(at, whole, slab, left, right):
    K, D = left.shape[:2]
    W = slab.shape[1]
    rows = jax.ShapeDtypeStruct((K * W * D, D), F32)
    return call(
        functools.partial(leaf_side_kernel, D, W, K),
        "leaf_side",
        24,
        0.7,
        (rows, rows),
        [SMEM, HBM, VMEM, VMEM, VMEM],
        (VMEM, VMEM),
        [pltpu.VMEM((D * D, D), F32), pltpu.VMEM((W * D, D), F32), pltpu.SemaphoreType.DMA((CHUNKS,))],
    )(at.reshape(1), whole.reshape(D * D, D), slab.reshape(D * W, D), left, right)


def leaf_rows(whole, sides, above):
    K, D = above.shape[:2]
    W = sides[0].shape[0] // (K * D)
    rows = pltpu.VMEM((K * W * D, D), F32)
    return call(
        functools.partial(leaf_kernel, D, W, K),
        "leaf",
        24,
        0.7,
        jax.ShapeDtypeStruct((K, 2, W, D), F32),
        [HBM, VMEM, VMEM, VMEM],
        VMEM,
        [pltpu.VMEM((D * D, D), F32), rows, rows, pltpu.SemaphoreType.DMA((CHUNKS,))],
    )(whole.reshape(D * D, D), sides[0], sides[1], above)


NODE = ("ylo", "zhi", "zlo")
BOND = ("yhi", "x", "core")
SLOT_OF = (4, 2, 5, 1, 6, 3, 7, 0)


def ein(spec, a, b):
    return jnp.einsum(spec, a, b, precision=lax.Precision.HIGHEST)


def after(x, other):
    return lax.optimization_barrier((x, other))[0]


def other_core(x):
    return lax.ppermute(x, "core", [(0, 1), (1, 0)])


def join_cores(half, core, axis):
    other = other_core(half)
    low = jnp.where(core == 0, half, other)
    high = jnp.where(core == 0, other, half)
    return jnp.concatenate([low, high], axis=axis)


def reorder_kernel(in_ref, out_ref):
    for g, s in enumerate(SLOT_OF):
        out_ref[g] = in_ref[s]


def reordered(x):
    return pl.pallas_call(
        reorder_kernel,
        out_shape=jax.ShapeDtypeStruct(x.shape, x.dtype),
        in_specs=[VMEM],
        out_specs=VMEM,
        compiler_params=pltpu.CompilerParams(vmem_limit_bytes=8 << 20),
        name="reorder",
    )(x)


def local(bottom_nodes, upper_nodes, leaf_up, outside_env, top_env):
    group = lax.axis_index(NODE)
    bond = lax.axis_index(BOND)
    core = lax.axis_index("core")
    yhi = lax.axis_index("yhi")
    op = jnp.minimum(lax.axis_index("x"), 2)
    width = bottom_nodes.shape[2]
    rows = bottom_nodes.shape[1]
    parts = width // rows

    got = lax.all_to_all(reordered(upper_nodes), NODE, 0, 0, tiled=True)
    shard = jnp.moveaxis(got, 0, 1).reshape(rows, width, width)
    upper = lax.all_gather(shard, BOND, axis=0, tiled=True)

    mine = bottom_nodes[0]
    left_leaf = leaf_up[0, :, 0]
    right_leaf = leaf_up[0, :, 1]
    middle = ein("kac,pcd->kpad", left_leaf, after(mine, shard))
    product = ein("kpad,kbd->kpab", middle, right_leaf)
    both = jnp.concatenate([mine[None], product])
    both = jnp.moveaxis(both.reshape(4, rows, parts, rows, width), 2, 0)
    both = lax.all_to_all(both, BOND, 0, 0, tiled=True)
    both = jnp.moveaxis(both, 1, 0).reshape(4, width, rows, width)
    mine_a = both[0]
    gram = ein("pab,kqab->kpq", mine_a, both[1:])
    pieces = jnp.moveaxis(gram.reshape(3, parts, rows, width), 1, 0)
    pieces = lax.all_to_all(pieces, BOND, 0, 0, tiled=True)
    env = jnp.sum(pieces, axis=0)
    by_x = jnp.stack([env[0], env[1], env[2], env[2]])
    by_dest = jnp.broadcast_to(by_x[None, None, :, None], (2, 2, 4, 2, rows, width))
    by_dest = by_dest.reshape(2 * parts, rows, width)
    pair = lax.all_to_all(by_dest, ("zlo",) + BOND, 0, 0, tiled=True)
    left3, right3 = pair.reshape(2, width, width)

    def move(x, *pairs):
        return lax.ppermute(x, NODE, pairs)

    def place(active, which=jnp.int32(0)):
        return jnp.stack([core, which, active.astype(jnp.int32)])

    is_third = group % 2 == 0
    is_second = (group == 1) | (group == 5)
    is_first = group == 3

    whole = lax.all_gather(after(mine, left3), BOND, axis=0, tiled=True)
    sides = leaf_sides(bond, whole, mine_a, left_leaf, right_leaf)

    up2 = up_rows(place(is_third), upper, left3, right3)
    ends = jnp.stack([move(up2, (0, 1), (4, 5)), move(up2, (2, 1), (6, 5))])
    left2, right2 = join_cores(ends, core, 1)
    top = lax.dynamic_index_in_dim(top_env, op, 0, keepdims=False)
    outside = lax.dynamic_index_in_dim(outside_env, op, 0, keepdims=False)
    at_crown = place(group == 7)
    crown = down_part(at_crown, upper, side_part(at_crown, upper, outside, outside), top)
    crown = move(crown, (7, 3))
    crown = crown + other_core(crown)
    side3 = side_part(place(is_third, yhi), upper, left3, right3)
    left2, right2, side3 = lax.optimization_barrier((left2, right2, side3))
    up1 = up_rows(place(is_second), upper, left2, right2)
    ends = jnp.stack([move(up1, (1, 3)), move(up1, (5, 3))])
    left1, right1 = join_cores(ends, core, 1)
    side2 = side_part(place(is_second, yhi), upper, left2, right2)
    left1, right1, side2 = lax.optimization_barrier((left1, right1, side2))

    def hand_down(x, *families):
        straight = []
        across = []
        for parent, one, two in families:
            straight += [(2 * parent, 2 * one), (2 * parent + 1, 2 * two + 1)]
            across += [(2 * parent, 2 * one + 1), (2 * parent + 1, 2 * two)]
        axes = NODE + ("yhi",)
        both = lax.ppermute(x, axes, straight) + lax.ppermute(x, axes, across)
        return both + other_core(both)

    at_first = place(is_first, yhi)
    side1 = side_part(at_first, upper, left1, right1)
    made = down_part(at_first, upper, side1, crown)
    above = hand_down(made, (3, 1, 5))
    root = up_rows(place(is_first), upper, left1, after(right1, made))
    made = down_part(place(is_second, yhi), upper, side2, above)
    above = hand_down(made, (1, 0, 2), (5, 4, 6))
    above, sides = lax.optimization_barrier((above, sides))
    made = down_part(place(is_third, yhi), upper, side3, above)
    straight = [(2 * g + 1, 2 * g + 3) for g in (0, 2, 4, 6)]
    across = [(2 * g + 1, 2 * g + 2) for g in (0, 2, 4, 6)]
    straight += [(2 * g, 2 * g + 1) for g in (0, 2, 4, 6)]
    axes = NODE + ("yhi",)
    last = lax.ppermute(made, axes, straight) + lax.ppermute(made, axes, across)
    last = last + jnp.where(is_third & (yhi == 0), made, 0.0)
    last = last + other_core(last)

    root = root + move(root, (3, 7))
    root = root + move(root, (3, 1), (7, 5))
    root = root + move(root, (3, 2), (1, 0), (7, 6), (5, 4))
    root = join_cores(root, core, 0)
    ends = lax.all_gather(jnp.stack([last, root]), "x", axis=0, tiled=False)
    above = ends[:3, 0]
    root_env = ends[:3, 1]

    return leaf_rows(whole, sides, above)[None], root_env


def solution(mesh):
    shape = (2, 2, 2, 2, 4, 2)
    fine = Mesh(mesh.devices.reshape(shape), NODE + BOND)
    placed = (
        P(NODE, BOND, None, None),
        P(None, BOND, NODE, None),
        P(NODE, None, None, None, None),
        P(),
        P(),
    )
    return jax.shard_map(
        local,
        mesh=fine,
        in_specs=placed,
        out_specs=(P(NODE, None, None, BOND, None), P()),
        check_vma=False,
    )
```

```python
import functools

import jax
import jax.numpy as jnp
from jax import lax
from jax.experimental import pallas as pl
from jax.experimental.pallas import tpu as pltpu
from jax.sharding import Mesh, PartitionSpec as P

BF = jnp.bfloat16
F32 = jnp.float32
CHUNKS = 8


def split(v):
    hi = v.astype(BF)
    return hi, (v - hi.astype(F32)).astype(BF)


def wide(v):
    return jnp.concatenate(split(v), axis=1)


def stacked(v):
    row = wide(v)
    return jnp.concatenate([row, row], axis=0)


def mm(a, b):
    return jnp.dot(a, b, preferred_element_type=F32)


def mm_t(a, b):
    return lax.dot_general(a, b, (((1,), (1,)), ((), ())), preferred_element_type=F32)


def fold(v):
    half = v.shape[1] // 2
    return v[:, :half] + v[:, half:]


def product(a_wide, b_stacked):
    return fold(mm(a_wide, b_stacked))


def pair_rows(one, two):
    h1, l1 = split(one)
    h2, l2 = split(two)
    return jnp.concatenate([jnp.concatenate([h1, h2], 1), jnp.concatenate([l1, l2], 1)], 0)


def quarters(acc):
    r = acc.shape[0] // 2
    c = acc.shape[1] // 2
    return (acc[:r, :c] + acc[r:, :c]) + (acc[:r, c:] + acc[r:, c:])


def aligned(i, n):
    return pl.multiple_of(i * n, n)


def fetch(src, dst, sems, count, first=0):
    size = dst.shape[0] // count

    def copy(i):
        at = lax.rem(first + i, count)
        there = pl.ds(aligned(at, size), size)
        return pltpu.make_async_copy(src.at[there], dst.at[there], sems.at[i])

    return copy


def up_kernel(D, H, place_ref, x_hbm, l_ref, r_ref, out_ref, x_ref, n_scr, sems):
    @pl.when(place_ref[2] == 0)
    def _():
        out_ref[...] = jnp.zeros_like(out_ref)

    @pl.when(place_ref[2] == 1)
    def _():
        count = 2 * CHUNKS
        copy = fetch(x_hbm, x_ref, sems, count, place_ref[0] * CHUNKS)
        for i in range(count):
            copy(i).start()
        start = place_ref[0] * H
        rr = stacked(r_ref[...])
        ll = wide(l_ref[...].T)
        per = H // CHUNKS

        def chunk(i, carry):
            copy(i).wait()
            for j in range(per):
                p = i * per + j
                t = product(wide(x_ref[pl.ds(aligned(start + p, D), D), :]), rr)
                n_scr[pl.ds(p, D, stride=H), :] = product(ll, stacked(t))
            return carry

        lax.fori_loop(0, CHUNKS, chunk, 0)
        for i in range(CHUNKS, count):
            copy(i).wait()

        def gram(i, acc):
            c = 2 * i
            lhs = pair_rows(n_scr[pl.ds(aligned(c, H), H), :], n_scr[pl.ds(aligned(c + 1, H), H), :])
            rhs = pair_rows(x_ref[pl.ds(c, D, stride=D), :], x_ref[pl.ds(c + 1, D, stride=D), :])
            return acc + mm_t(lhs, rhs)

        acc = lax.fori_loop(0, D // 2, gram, jnp.zeros((2 * H, 2 * D), F32), unroll=8)
        out_ref[...] = quarters(acc)


def side_kernel(D, H, place_ref, x_hbm, l_ref, r_ref, s_hbm, x_ref, s_ref, sems):
    @pl.when(place_ref[2] == 1)
    def _():
        copy = fetch(x_hbm, x_ref, sems, CHUNKS)
        for i in range(CHUNKS):
            copy(i).start()
        start = place_ref[0] * H
        per = D // CHUNKS

        @pl.when(place_ref[1] == 0)
        def _():
            rr = stacked(r_ref[...])

            def chunk(i, carry):
                copy(i).wait()
                for j in range(per):
                    p = i * per + j
                    x = x_ref[pl.ds(aligned(2 * p + place_ref[0], H), H), :]
                    s_ref[pl.ds(p, H, stride=D), :] = product(wide(x), rr)
                return carry

            lax.fori_loop(0, CHUNKS, chunk, 0)

        @pl.when(place_ref[1] == 1)
        def _():
            ll = wide(l_ref[...].T)
            half = jnp.where(place_ref[0] == 0, ll[:H], ll[H:])

            def chunk(i, carry):
                copy(i).wait()
                for j in range(per):
                    p = i * per + j
                    x = x_ref[pl.ds(aligned(p, D), D), :]
                    s_ref[pl.ds(p, H, stride=D), :] = product(half, stacked(x))
                return carry

            lax.fori_loop(0, CHUNKS, chunk, 0)

        done = pltpu.make_async_copy(s_ref, s_hbm, sems.at[0])
        done.start()
        done.wait()


def down_kernel(D, H, place_ref, x_hbm, s_hbm, e_ref, out_ref, x_ref, s_ref, n_scr, sems):
    out_ref[...] = jnp.zeros_like(out_ref)

    @pl.when(place_ref[2] == 1)
    def _():
        s_copy = fetch(s_hbm, s_ref, sems, CHUNKS)
        x_copy = fetch(x_hbm, x_ref, sems.at[pl.ds(CHUNKS, CHUNKS)], CHUNKS)
        for i in range(CHUNKS):
            s_copy(i).start()
        for i in range(CHUNKS):
            x_copy(i).start()
        start = place_ref[0] * H
        ee = wide(e_ref[...].T)
        per = H // CHUNKS

        def chunk(i, carry):
            s_copy(i).wait()
            for j in range(per):
                v = i * per + j
                t = s_ref[pl.ds(aligned(v, D), D), :]
                n_scr[pl.ds(v, D, stride=H), :] = product(ee, stacked(t))
            return carry

        lax.fori_loop(0, CHUNKS, chunk, 0)
        for i in range(CHUNKS):
            x_copy(i).wait()

        @pl.when(place_ref[1] == 0)
        def _():
            def gram(i, acc):
                q = 2 * i
                lhs = pair_rows(n_scr[pl.ds(aligned(q, H), H), :], n_scr[pl.ds(aligned(q + 1, H), H), :])
                rhs = pair_rows(x_ref[pl.ds(aligned(q, D), D), :], x_ref[pl.ds(aligned(q + 1, D), D), :])
                return acc + mm_t(lhs, rhs)

            acc = lax.fori_loop(0, D // 2, gram, jnp.zeros((2 * H, 2 * D), F32), unroll=8)
            out_ref[pl.ds(aligned(place_ref[0], H), H), :] = quarters(acc)

        @pl.when(place_ref[1] == 1)
        def _():
            def gram(i, acc):
                q = 4 * i
                v = n_scr[pl.ds(aligned(i, 4 * H), 4 * H), :].T
                lhs = jnp.concatenate(split(v), 0)
                x = [x_ref[pl.ds(pl.multiple_of((q + j) * D + start, H), H), :] for j in range(4)]
                return acc + mm(lhs, wide(jnp.concatenate(x, 0)))

            acc = lax.fori_loop(0, D // 4, gram, jnp.zeros((2 * D, 2 * D), F32), unroll=4)
            out_ref[...] = quarters(acc)


def leaf_side_kernel(D, W, K, at_ref, x_hbm, xa_ref, l_ref, r_ref, t_ref, u_ref, x_ref, b_scr, sems):
    copy = fetch(x_hbm, x_ref, sems, CHUNKS)
    for i in range(CHUNKS):
        copy(i).start()
    for k in range(K):
        rr = stacked(r_ref[k])
        for a in range(W):
            x = xa_ref[pl.ds(a, D, stride=W), :]
            t_ref[pl.ds((k * W + a) * D, D), :] = product(wide(x), rr)
    lane = lax.broadcasted_iota(jnp.int32, (W, D), 1)
    line = lax.broadcasted_iota(jnp.int32, (W, D), 0)
    pick = jnp.where(lane == line + at_ref[0] * W, 1.0, 0.0).astype(BF)
    per = D // CHUNKS

    def chunk(i, carry):
        copy(i).wait()
        for j in range(per):
            p = i * per + j
            x = x_ref[pl.ds(aligned(p, D), D), :]
            b_scr[pl.ds(p, W, stride=D), :] = fold(mm_t(pick, jnp.concatenate(split(x), 0)))
        return carry

    lax.fori_loop(0, CHUNKS, chunk, 0)
    for k in range(K):
        ll = stacked(l_ref[k])
        for b in range(W):
            u_ref[pl.ds((k * W + b) * D, D), :] = product(wide(b_scr[pl.ds(b * D, D), :]), ll)


def leaf_kernel(D, W, K, x_hbm, t_ref, u_ref, e_ref, out_ref, x_ref, n_scr, v_scr, sems):
    copy = fetch(x_hbm, x_ref, sems, CHUNKS)
    for i in range(CHUNKS):
        copy(i).start()
    R = K * W
    for k in range(K):
        ee = wide(e_ref[k].T)
        for w in range(W):
            r = k * W + w
            n_scr[pl.ds(r, D, stride=R), :] = product(ee, stacked(t_ref[pl.ds(r * D, D), :]))
            v_scr[pl.ds(r, D, stride=R), :] = product(ee, stacked(u_ref[pl.ds(r * D, D), :]))
    for i in range(CHUNKS):
        copy(i).wait()

    def gram(i, accs):
        q = 2 * i
        one, two = pl.ds(aligned(q, R), R), pl.ds(aligned(q + 1, R), R)
        h1, l1 = split(x_ref[pl.ds(aligned(q, D), D), :])
        h2, l2 = split(x_ref[pl.ds(aligned(q + 1, D), D), :])
        cat = jnp.concatenate
        by_last = cat([cat([h1, h2], 1), cat([l1, l2], 1)], 0)
        by_first = cat([cat([h1, l1], 1), cat([h2, l2], 1)], 0)
        first = mm_t(pair_rows(n_scr[one, :], n_scr[two, :]), by_last)
        second = mm(pair_rows(v_scr[one, :], v_scr[two, :]), by_first)
        return accs[0] + first, accs[1] + second

    zero = jnp.zeros((2 * R, 2 * D), F32)
    first, second = lax.fori_loop(0, D // 2, gram, (zero, zero), unroll=4)
    first = quarters(first)
    second = quarters(second)
    for k in range(K):
        out_ref[k, 0] = first[k * W : (k + 1) * W]
        out_ref[k, 1] = second[k * W : (k + 1) * W]


VMEM = pl.BlockSpec(memory_space=pltpu.VMEM)
SMEM = pl.BlockSpec(memory_space=pltpu.SMEM)
HBM = pl.BlockSpec(memory_space=pltpu.HBM)


def call(kernel, name, mib, units, out_shape, in_specs, out_specs, scratch):
    return pl.pallas_call(
        kernel,
        out_shape=out_shape,
        in_specs=in_specs,
        out_specs=out_specs,
        scratch_shapes=scratch,
        compiler_params=pltpu.CompilerParams(vmem_limit_bytes=57 << 20),
        cost_estimate=pl.CostEstimate(
            flops=int(units * 4.8e9), bytes_accessed=8 << 20, transcendentals=0
        ),
        name=name,
    )


def up_rows(place, tensor, left_env, right_env):
    D = left_env.shape[0]
    H = D // 2
    return call(
        functools.partial(up_kernel, D, H),
        "up",
        24,
        1,
        jax.ShapeDtypeStruct((H, D), F32),
        [SMEM, HBM, VMEM, VMEM],
        VMEM,
        [pltpu.VMEM((D * D, D), F32), pltpu.VMEM((D * H, D), F32), pltpu.SemaphoreType.DMA((2 * CHUNKS,))],
    )(place, tensor.reshape(D * D, D), left_env, right_env)


def side_part(place, tensor, left_env, right_env):
    D = left_env.shape[0]
    H = D // 2
    return call(
        functools.partial(side_kernel, D, H),
        "side",
        24,
        0.4,
        jax.ShapeDtypeStruct((D * H, D), F32),
        [SMEM, HBM, VMEM, VMEM],
        HBM,
        [pltpu.VMEM((D * D, D), F32), pltpu.VMEM((D * H, D), F32), pltpu.SemaphoreType.DMA((CHUNKS,))],
    )(place, tensor.reshape(D * D, D), left_env, right_env)


def down_part(place, tensor, side, above):
    D = above.shape[0]
    H = D // 2
    big = pltpu.VMEM((D * D, D), F32)
    half = pltpu.VMEM((D * H, D), F32)
    return call(
        functools.partial(down_kernel, D, H),
        "down",
        28,
        0.7,
        jax.ShapeDtypeStruct((D, D), F32),
        [SMEM, HBM, HBM, VMEM],
        VMEM,
        [big, half, half, pltpu.SemaphoreType.DMA((2 * CHUNKS,))],
    )(place, tensor.reshape(D * D, D), side, above)


def leaf_sides(at, whole, slab, left, right):
    K, D = left.shape[:2]
    W = slab.shape[1]
    rows = jax.ShapeDtypeStruct((K * W * D, D), F32)
    return call(
        functools.partial(leaf_side_kernel, D, W, K),
        "leaf_side",
        24,
        0.7,
        (rows, rows),
        [SMEM, HBM, VMEM, VMEM, VMEM],
        (VMEM, VMEM),
        [pltpu.VMEM((D * D, D), F32), pltpu.VMEM((W * D, D), F32), pltpu.SemaphoreType.DMA((CHUNKS,))],
    )(at.reshape(1), whole.reshape(D * D, D), slab.reshape(D * W, D), left, right)


def leaf_rows(whole, sides, above):
    K, D = above.shape[:2]
    W = sides[0].shape[0] // (K * D)
    rows = pltpu.VMEM((K * W * D, D), F32)
    return call(
        functools.partial(leaf_kernel, D, W, K),
        "leaf",
        24,
        0.7,
        jax.ShapeDtypeStruct((K, 2, W, D), F32),
        [HBM, VMEM, VMEM, VMEM],
        VMEM,
        [pltpu.VMEM((D * D, D), F32), rows, rows, pltpu.SemaphoreType.DMA((CHUNKS,))],
    )(whole.reshape(D * D, D), sides[0], sides[1], above)


NODE = ("ylo", "zhi", "zlo")
BOND = ("yhi", "x", "core")
SLOT_OF = (4, 2, 5, 1, 6, 3, 7, 0)


def ein(spec, a, b):
    return jnp.einsum(spec, a, b, precision=lax.Precision.HIGHEST)


def after(x, other):
    return lax.optimization_barrier((x, other))[0]


def other_core(x):
    return lax.ppermute(x, "core", [(0, 1), (1, 0)])


def join_cores(half, core, axis):
    other = other_core(half)
    low = jnp.where(core == 0, half, other)
    high = jnp.where(core == 0, other, half)
    return jnp.concatenate([low, high], axis=axis)


def reorder_kernel(in_ref, out_ref):
    for g, s in enumerate(SLOT_OF):
        out_ref[g] = in_ref[s]


def reordered(x):
    return pl.pallas_call(
        reorder_kernel,
        out_shape=jax.ShapeDtypeStruct(x.shape, x.dtype),
        in_specs=[VMEM],
        out_specs=VMEM,
        compiler_params=pltpu.CompilerParams(vmem_limit_bytes=8 << 20),
        name="reorder",
    )(x)


def local(bottom_nodes, upper_nodes, leaf_up, outside_env, top_env):
    group = lax.axis_index(NODE)
    bond = lax.axis_index(BOND)
    core = lax.axis_index("core")
    yhi = lax.axis_index("yhi")
    op = jnp.minimum(lax.axis_index("x"), 2)
    width = bottom_nodes.shape[2]
    rows = bottom_nodes.shape[1]
    parts = width // rows

    got = lax.all_to_all(reordered(upper_nodes), NODE, 0, 0, tiled=True)
    shard = jnp.moveaxis(got, 0, 1).reshape(rows, width, width)
    upper = lax.all_gather(shard, BOND, axis=0, tiled=True)

    mine = bottom_nodes[0]
    left_leaf = leaf_up[0, :, 0]
    right_leaf = leaf_up[0, :, 1]
    middle = ein("kac,pcd->kpad", left_leaf, after(mine, shard))
    product = ein("kpad,kbd->kpab", middle, right_leaf)
    both = jnp.concatenate([mine[None], product])
    both = jnp.moveaxis(both.reshape(4, rows, parts, rows, width), 2, 0)
    both = lax.all_to_all(both, BOND, 0, 0, tiled=True)
    both = jnp.moveaxis(both, 1, 0).reshape(4, width, rows, width)
    mine_a = both[0]
    gram = ein("pab,kqab->kpq", mine_a, both[1:])
    pieces = jnp.moveaxis(gram.reshape(3, parts, rows, width), 1, 0)
    pieces = lax.all_to_all(pieces, BOND, 0, 0, tiled=True)
    env = jnp.sum(pieces, axis=0)
    by_x = jnp.stack([env[0], env[1], env[2], env[2]])
    by_dest = jnp.broadcast_to(by_x[None, None, :, None], (2, 2, 4, 2, rows, width))
    by_dest = by_dest.reshape(2 * parts, rows, width)
    pair = lax.all_to_all(by_dest, ("zlo",) + BOND, 0, 0, tiled=True)
    left3, right3 = pair.reshape(2, width, width)

    def move(x, *pairs):
        return lax.ppermute(x, NODE, pairs)

    def place(active, which=jnp.int32(0)):
        return jnp.stack([core, which, active.astype(jnp.int32)])

    is_third = group % 2 == 0
    is_second = (group == 1) | (group == 5)
    is_first = group == 3

    whole = lax.all_gather(after(mine, left3), BOND, axis=0, tiled=True)
    sides = leaf_sides(bond, whole, mine_a, left_leaf, right_leaf)

    up2 = up_rows(place(is_third), upper, left3, right3)
    ends = jnp.stack([move(up2, (0, 1), (4, 5)), move(up2, (2, 1), (6, 5))])
    left2, right2 = join_cores(ends, core, 1)
    top = lax.dynamic_index_in_dim(top_env, op, 0, keepdims=False)
    outside = lax.dynamic_index_in_dim(outside_env, op, 0, keepdims=False)
    at_crown = place(group == 7)
    crown = down_part(at_crown, upper, side_part(at_crown, upper, outside, outside), top)
    crown = move(crown, (7, 3))
    crown = crown + other_core(crown)
    side3 = side_part(place(is_third, yhi), upper, left3, right3)
    left2, right2, side3 = lax.optimization_barrier((left2, right2, side3))
    up1 = up_rows(place(is_second), upper, left2, right2)
    ends = jnp.stack([move(up1, (1, 3)), move(up1, (5, 3))])
    left1, right1 = join_cores(ends, core, 1)
    side2 = side_part(place(is_second, yhi), upper, left2, right2)
    left1, right1, side2 = lax.optimization_barrier((left1, right1, side2))

    def send_both(x, straight, across):
        axes = NODE + ("yhi",)
        return lax.ppermute(x, axes, straight), lax.ppermute(x, axes, across)

    def family(parent, one, two):
        straight = [(2 * parent, 2 * one), (2 * parent + 1, 2 * two + 1)]
        across = [(2 * parent, 2 * one + 1), (2 * parent + 1, 2 * two)]
        return straight, across

    at_first = place(is_first, yhi)
    side1 = side_part(at_first, upper, left1, right1)
    made = down_part(at_first, upper, side1, crown)
    one, two = send_both(made, *family(3, 1, 5))
    above = one + two
    above = above + other_core(above)
    root = up_rows(place(is_first), upper, left1, after(right1, made))
    root = join_cores(root, core, 0)
    made = down_part(place(is_second, yhi), upper, side2, above)

    fa, fb = family(1, 0, 2), family(5, 4, 6)
    one, two = send_both(
        jnp.where(is_first, root, made),
        fa[0] + fb[0] + [(6, 14), (7, 15)],
        fa[1] + fb[1] + [(6, 2), (7, 3)],
    )
    one, two, *sides = lax.optimization_barrier((one, two, *sides))
    root = jnp.where(group == 7, one, jnp.where(group == 1, two, root))
    above = one + two
    above = above + other_core(above)
    made = down_part(place(is_third, yhi), upper, side3, above)
    straight = [(1, 3), (5, 7), (9, 11), (13, 15), (0, 1), (4, 5), (8, 9), (12, 13)]
    across = [(1, 2), (5, 6), (9, 10), (13, 14)]
    straight += [(2, 0), (3, 4), (6, 8), (14, 12), (15, 10)]
    across += [(2, 1), (3, 5), (6, 9), (14, 13), (15, 11)]
    one, two = send_both(jnp.where(is_third, made, root), straight, across)
    has_root = (group == 1) | (group == 3) | (group == 7)
    root = jnp.where(has_root, root, jnp.where(yhi == 0, one, two))
    kept = jnp.where(is_third, made, two)
    last = jnp.where(yhi == 0, kept, one)
    last = last + other_core(last)
    ends = lax.all_gather(jnp.stack([last, root]), "x", axis=0, tiled=False)
    above = ends[:3, 0]
    root_env = ends[:3, 1]
    return leaf_rows(whole, sides, above)[None], root_env


def solution(mesh):
    shape = (2, 2, 2, 2, 4, 2)
    fine = Mesh(mesh.devices.reshape(shape), NODE + BOND)
    placed = (
        P(NODE, BOND, None, None),
        P(None, BOND, NODE, None),
        P(NODE, None, None, None, None),
        P(),
        P(),
    )
    return jax.shard_map(
        local,
        mesh=fine,
        in_specs=placed,
        out_specs=(P(NODE, None, None, BOND, None), P()),
        check_vma=False,
    )
```

```python
import functools

import jax
import jax.numpy as jnp
from jax import lax
from jax.experimental import pallas as pl
from jax.experimental.pallas import tpu as pltpu
from jax.sharding import Mesh, PartitionSpec as P

BF = jnp.bfloat16
F32 = jnp.float32
CHUNKS = 8


def split(v):
    hi = v.astype(BF)
    return hi, (v - hi.astype(F32)).astype(BF)


def wide(v):
    return jnp.concatenate(split(v), axis=1)


def stacked(v):
    row = wide(v)
    return jnp.concatenate([row, row], axis=0)


def mm(a, b):
    return jnp.dot(a, b, preferred_element_type=F32)


def mm_t(a, b):
    return lax.dot_general(a, b, (((1,), (1,)), ((), ())), preferred_element_type=F32)


def fold(v):
    half = v.shape[1] // 2
    return v[:, :half] + v[:, half:]


def product(a_wide, b_stacked):
    return fold(mm(a_wide, b_stacked))


def pair_rows(one, two):
    h1, l1 = split(one)
    h2, l2 = split(two)
    return jnp.concatenate([jnp.concatenate([h1, h2], 1), jnp.concatenate([l1, l2], 1)], 0)


def quarters(acc):
    r = acc.shape[0] // 2
    c = acc.shape[1] // 2
    return (acc[:r, :c] + acc[r:, :c]) + (acc[:r, c:] + acc[r:, c:])


def aligned(i, n):
    return pl.multiple_of(i * n, n)


def chunks_of(src, dst, sems):
    size = dst.shape[0] // CHUNKS

    def copy(i):
        there = pl.ds(aligned(i, size), size)
        return pltpu.make_async_copy(src.at[there], dst.at[there], sems.at[i])

    return copy


def up_kernel(D, H, place_ref, x_ref, l_ref, r_ref, out_ref, n_scr):
    @pl.when(place_ref[2] == 0)
    def _():
        out_ref[...] = jnp.zeros_like(out_ref)

    @pl.when(place_ref[2] == 1)
    def _():
        start = place_ref[0] * H
        rr = stacked(r_ref[...])
        ll = wide(l_ref[...].T)

        def slab(p, carry):
            t = product(wide(x_ref[pl.ds(aligned(start + p, D), D), :]), rr)
            n_scr[pl.ds(p, D, stride=H), :] = product(ll, stacked(t))
            return carry

        lax.fori_loop(0, H, slab, 0, unroll=8)

        def gram(i, acc):
            c = 2 * i
            lhs = pair_rows(n_scr[pl.ds(aligned(c, H), H), :], n_scr[pl.ds(aligned(c + 1, H), H), :])
            rhs = pair_rows(x_ref[pl.ds(c, D, stride=D), :], x_ref[pl.ds(c + 1, D, stride=D), :])
            return acc + mm_t(lhs, rhs)

        acc = lax.fori_loop(0, D // 2, gram, jnp.zeros((2 * H, 2 * D), F32), unroll=8)
        out_ref[...] = quarters(acc)


def side_kernel(D, H, place_ref, x_ref, l_ref, r_ref, s_ref):
    @pl.when((place_ref[2] == 1) & (place_ref[1] == 0))
    def _():
        rr = stacked(r_ref[...])

        def slab(p, carry):
            x = x_ref[pl.ds(aligned(2 * p + place_ref[0], H), H), :]
            s_ref[pl.ds(p, H, stride=D), :] = product(wide(x), rr)
            return carry

        lax.fori_loop(0, D, slab, 0, unroll=8)

    @pl.when((place_ref[2] == 1) & (place_ref[1] == 1))
    def _():
        ll = wide(l_ref[...].T)
        half = jnp.where(place_ref[0] == 0, ll[:H], ll[H:])

        def slab(p, carry):
            x = x_ref[pl.ds(aligned(p, D), D), :]
            s_ref[pl.ds(p, H, stride=D), :] = product(half, stacked(x))
            return carry

        lax.fori_loop(0, D, slab, 0, unroll=8)


def down_kernel(D, H, stream, place_ref, x_ref, s_ref, e_ref, out_ref, n_scr, *own):
    out_ref[...] = jnp.zeros_like(out_ref)
    if stream:
        x_hbm, s_hbm = x_ref, s_ref
        x_ref, s_ref, x_sems, s_sems = own
        x_copy = chunks_of(x_hbm, x_ref, x_sems)
        s_copy = chunks_of(s_hbm, s_ref, s_sems)

    @pl.when(place_ref[2] == 1)
    def _():
        if stream:
            for i in range(CHUNKS):
                s_copy(i).start()
            for i in range(CHUNKS):
                x_copy(i).start()
        start = place_ref[0] * H
        ee = wide(e_ref[...].T)
        per = H // CHUNKS

        def chunk(i, carry):
            if stream:
                s_copy(i).wait()
            for j in range(per):
                v = i * per + j
                t = s_ref[pl.ds(aligned(v, D), D), :]
                n_scr[pl.ds(v, D, stride=H), :] = product(ee, stacked(t))
            return carry

        lax.fori_loop(0, CHUNKS, chunk, 0)
        if stream:
            for i in range(CHUNKS):
                x_copy(i).wait()

        @pl.when(place_ref[1] == 0)
        def _():
            def gram(i, acc):
                q = 2 * i
                lhs = pair_rows(n_scr[pl.ds(aligned(q, H), H), :], n_scr[pl.ds(aligned(q + 1, H), H), :])
                rhs = pair_rows(x_ref[pl.ds(aligned(q, D), D), :], x_ref[pl.ds(aligned(q + 1, D), D), :])
                return acc + mm_t(lhs, rhs)

            acc = lax.fori_loop(0, D // 2, gram, jnp.zeros((2 * H, 2 * D), F32), unroll=8)
            out_ref[pl.ds(aligned(place_ref[0], H), H), :] = quarters(acc)

        @pl.when(place_ref[1] == 1)
        def _():
            def gram(i, acc):
                q = 4 * i
                v = n_scr[pl.ds(aligned(i, 4 * H), 4 * H), :].T
                lhs = jnp.concatenate(split(v), 0)
                x = [x_ref[pl.ds(pl.multiple_of((q + j) * D + start, H), H), :] for j in range(4)]
                return acc + mm(lhs, wide(jnp.concatenate(x, 0)))

            acc = lax.fori_loop(0, D // 4, gram, jnp.zeros((2 * D, 2 * D), F32), unroll=4)
            out_ref[...] = quarters(acc)


def leaf_side_kernel(D, B, W, at_ref, x_ref, l_ref, r_ref, t_ref, u_ref, b_scr):
    rr = stacked(r_ref[...])
    ll = stacked(l_ref[...])

    def first(r, carry):
        a = at_ref[0] + lax.div(r, W) * at_ref[1] + lax.rem(r, W)
        x = x_ref[pl.ds(a, D, stride=D), :]
        t_ref[pl.ds(aligned(r, D), D), :] = product(wide(x), rr)
        return carry

    lax.fori_loop(0, B * W, first, 0, unroll=8)
    lane = lax.broadcasted_iota(jnp.int32, (W, D), 1)
    line = lax.broadcasted_iota(jnp.int32, (W, D), 0)
    pick = jnp.concatenate(
        [jnp.where(lane == line + at_ref[0] + j * at_ref[1], 1.0, 0.0) for j in range(B)], 0
    ).astype(BF)

    def turn(p, carry):
        x = x_ref[pl.ds(aligned(p, D), D), :]
        b_scr[pl.ds(p, B * W, stride=D), :] = fold(mm_t(pick, jnp.concatenate(split(x), 0)))
        return carry

    lax.fori_loop(0, D, turn, 0, unroll=8)

    def second(r, carry):
        at = pl.ds(aligned(r, D), D)
        u_ref[at, :] = product(wide(b_scr[at, :]), ll)
        return carry

    lax.fori_loop(0, B * W, second, 0, unroll=8)


def leaf_kernel(D, R, x_hbm, t_ref, u_ref, e_ref, out_ref, x_ref, n_scr, v_scr, sems):
    copy = chunks_of(x_hbm, x_ref, sems)
    for i in range(CHUNKS):
        copy(i).start()
    ee = wide(e_ref[...].T)

    def slab(r, carry):
        at = pl.ds(aligned(r, D), D)
        n_scr[pl.ds(r, D, stride=R), :] = product(ee, stacked(t_ref[at, :]))
        v_scr[pl.ds(r, D, stride=R), :] = product(ee, stacked(u_ref[at, :]))
        return carry

    lax.fori_loop(0, R, slab, 0, unroll=4)
    for i in range(CHUNKS):
        copy(i).wait()

    def gram(i, accs):
        q = 2 * i
        one, two = pl.ds(aligned(q, R), R), pl.ds(aligned(q + 1, R), R)
        h1, l1 = split(x_ref[pl.ds(aligned(q, D), D), :])
        h2, l2 = split(x_ref[pl.ds(aligned(q + 1, D), D), :])
        cat = jnp.concatenate
        by_last = cat([cat([h1, h2], 1), cat([l1, l2], 1)], 0)
        by_first = cat([cat([h1, l1], 1), cat([h2, l2], 1)], 0)
        first = mm_t(pair_rows(n_scr[one, :], n_scr[two, :]), by_last)
        second = mm(pair_rows(v_scr[one, :], v_scr[two, :]), by_first)
        return accs[0] + first, accs[1] + second

    zero = jnp.zeros((2 * R, 2 * D), F32)
    first, second = lax.fori_loop(0, D // 2, gram, (zero, zero), unroll=4)
    out_ref[0] = quarters(first)
    out_ref[1] = quarters(second)


VMEM = pl.BlockSpec(memory_space=pltpu.VMEM)
HBM = pl.BlockSpec(memory_space=pltpu.HBM)
SMEM = pl.BlockSpec(memory_space=pltpu.SMEM)


def call(kernel, name, mib, units, out_shape, in_specs, out_specs, scratch):
    return pl.pallas_call(
        kernel,
        out_shape=out_shape,
        in_specs=in_specs,
        out_specs=out_specs,
        scratch_shapes=scratch,
        compiler_params=pltpu.CompilerParams(vmem_limit_bytes=mib << 20),
        cost_estimate=pl.CostEstimate(
            flops=int(units * 4.8e9), bytes_accessed=8 << 20, transcendentals=0
        ),
        name=name,
    )


def up_rows(place, tensor, left_env, right_env, cuts=2):
    D = left_env.shape[0]
    H = D // cuts
    return call(
        functools.partial(up_kernel, D, H),
        "up",
        28,
        1,
        jax.ShapeDtypeStruct((H, D), F32),
        [SMEM, VMEM, VMEM, VMEM],
        VMEM,
        [pltpu.VMEM((D * H, D), F32)],
    )(place, tensor.reshape(D * D, D), left_env, right_env)


def side_part(place, tensor, left_env, right_env):
    D = left_env.shape[0]
    H = D // 2
    return call(
        functools.partial(side_kernel, D, H),
        "side",
        28,
        0.4,
        jax.ShapeDtypeStruct((D * H, D), F32),
        [SMEM, VMEM, VMEM, VMEM],
        VMEM,
        [],
    )(place, tensor.reshape(D * D, D), left_env, right_env)


def down_part(place, tensor, side, above, stream=False):
    D = above.shape[0]
    H = D // 2
    big = HBM if stream else VMEM
    own = [
        pltpu.VMEM((D * D, D), F32),
        pltpu.VMEM((D * H, D), F32),
        pltpu.SemaphoreType.DMA((CHUNKS,)),
        pltpu.SemaphoreType.DMA((CHUNKS,)),
    ]
    return call(
        functools.partial(down_kernel, D, H, stream),
        "down",
        57 if stream else 28,
        0.7,
        jax.ShapeDtypeStruct((D, D), F32),
        [SMEM, big, big, VMEM],
        VMEM,
        [pltpu.VMEM((D * H, D), F32)] + (own if stream else []),
    )(place, tensor.reshape(D * D, D), side, above)


def leaf_sides(at, whole, left, right, blocks, width):
    D = left.shape[0]
    rows = jax.ShapeDtypeStruct((blocks * width * D, D), F32)
    return call(
        functools.partial(leaf_side_kernel, D, blocks, width),
        "leaf_side",
        28,
        0.7,
        (rows, rows),
        [SMEM, VMEM, VMEM, VMEM],
        (VMEM, VMEM),
        [pltpu.VMEM((blocks * width * D, D), F32)],
    )(at, whole.reshape(D * D, D), left, right)


def leaf_rows(whole, sides, above):
    D = above.shape[0]
    R = sides[0].shape[0] // D
    rows = pltpu.VMEM((R * D, D), F32)
    return call(
        functools.partial(leaf_kernel, D, R),
        "leaf",
        57,
        0.7,
        jax.ShapeDtypeStruct((2, R, D), F32),
        [HBM, VMEM, VMEM, VMEM],
        VMEM,
        [pltpu.VMEM((D * D, D), F32), rows, rows, pltpu.SemaphoreType.DMA((CHUNKS,))],
    )(whole.reshape(D * D, D), sides[0], sides[1], above)


NODE = ("ylo", "zhi", "zlo")
BOND = ("yhi", "x", "core")
SLOT_OF = (4, 2, 5, 1, 6, 3, 7, 0)


def ein(spec, a, b):
    return jnp.einsum(spec, a, b, precision=lax.Precision.HIGHEST)


def after(x, other):
    return lax.optimization_barrier((x, other))[0]


def other_core(x):
    return lax.ppermute(x, "core", [(0, 1), (1, 0)])


def join_cores(half, core, axis):
    other = other_core(half)
    low = jnp.where(core == 0, half, other)
    high = jnp.where(core == 0, other, half)
    return jnp.concatenate([low, high], axis=axis)


def reorder_kernel(in_ref, out_ref):
    for g, s in enumerate(SLOT_OF):
        out_ref[g] = in_ref[s]


def reordered(x):
    return pl.pallas_call(
        reorder_kernel,
        out_shape=jax.ShapeDtypeStruct(x.shape, x.dtype),
        in_specs=[VMEM],
        out_specs=VMEM,
        compiler_params=pltpu.CompilerParams(vmem_limit_bytes=8 << 20),
        name="reorder",
    )(x)


def local(bottom_nodes, upper_nodes, leaf_up, outside_env, top_env):
    group = lax.axis_index(NODE)
    core = lax.axis_index("core")
    yhi = lax.axis_index("yhi")
    op = jnp.minimum(lax.axis_index("x"), 2)
    width = bottom_nodes.shape[2]
    rows = bottom_nodes.shape[1]
    parts = width // rows

    got = lax.all_to_all(reordered(upper_nodes), NODE, 0, 0, tiled=True)
    shard = jnp.moveaxis(got, 0, 1).reshape(rows, width, width)
    upper = lax.all_gather(shard, BOND, axis=0, tiled=True)

    mine = bottom_nodes[0]
    left_leaf = leaf_up[0, :, 0]
    right_leaf = leaf_up[0, :, 1]
    middle = ein("kac,pcd->kpad", left_leaf, after(mine, shard))
    product = ein("kpad,kbd->kpab", middle, right_leaf)
    both = jnp.concatenate([mine[None], product])
    both = jnp.moveaxis(both.reshape(4, rows, parts, rows, width), 2, 0)
    both = lax.all_to_all(both, BOND, 0, 0, tiled=True)
    both = jnp.moveaxis(both, 1, 0).reshape(4, width, rows, width)
    mine_a = both[0]
    gram = ein("pab,kqab->kpq", mine_a, both[1:])
    pieces = jnp.moveaxis(gram.reshape(3, parts, rows, width), 1, 0)
    pieces = lax.all_to_all(pieces, BOND, 0, 0, tiled=True)
    env = jnp.sum(pieces, axis=0)
    by_x = jnp.stack([env[0], env[1], env[2], env[2]])
    by_dest = jnp.broadcast_to(by_x[None, None, :, None], (2, 2, 4, 2, rows, width))
    by_dest = by_dest.reshape(2 * parts, rows, width)
    pair = lax.all_to_all(by_dest, ("zlo",) + BOND, 0, 0, tiled=True)
    left3, right3 = pair.reshape(2, width, width)

    def move(x, *pairs):
        return lax.ppermute(x, NODE, pairs)

    def send_both(x, straight, across):
        axes = NODE + ("yhi",)
        return lax.ppermute(x, axes, straight), lax.ppermute(x, axes, across)

    def place(active, which=jnp.int32(0)):
        return jnp.stack([core, which, active.astype(jnp.int32)])

    is_third = group % 2 == 0
    is_second = (group == 1) | (group == 5)
    is_first = group == 3

    whole = lax.all_gather(after(mine, left3), BOND, axis=0, tiled=True)
    own_left = lax.dynamic_index_in_dim(left_leaf, op, 0, keepdims=False)
    own_right = lax.dynamic_index_in_dim(right_leaf, op, 0, keepdims=False)
    at = jnp.stack([(yhi * 8 + core) * rows, jnp.int32(2 * rows)])
    sides = leaf_sides(at, whole, own_left, own_right, 4, rows)

    up2 = up_rows(place(is_third), upper, left3, right3)
    ends = jnp.stack([move(up2, (0, 1), (4, 5)), move(up2, (2, 1), (6, 5))])
    left2, right2 = join_cores(ends, core, 1)
    top = lax.dynamic_index_in_dim(top_env, op, 0, keepdims=False)
    outside = lax.dynamic_index_in_dim(outside_env, op, 0, keepdims=False)
    at_crown = place(group == 7)
    crown = down_part(at_crown, upper, side_part(at_crown, upper, outside, outside), top)
    crown = move(crown, (7, 3))
    crown = crown + other_core(crown)
    side3 = side_part(place(is_third, yhi), upper, left3, right3)
    left2, right2, side3 = lax.optimization_barrier((left2, right2, side3))
    quarter = jnp.stack([2 * yhi + core, jnp.int32(0), is_second.astype(jnp.int32)])
    up1 = up_rows(quarter, upper, left2, right2, 4)
    one, two = send_both(up1, [(10, 6), (3, 7)], [(11, 6), (2, 7)])
    low = jnp.where(yhi == 0, one, two)
    high = jnp.where(yhi == 0, two, one)
    ends = join_cores(jnp.stack([low, high])[:, None], core, 1)
    only1 = ends.reshape(width, width)
    side2 = side_part(place(is_second, yhi), upper, left2, right2)
    only1, side2 = lax.optimization_barrier((only1, side2))

    def family(parent, one, two):
        straight = [(2 * parent, 2 * one), (2 * parent + 1, 2 * two + 1)]
        across = [(2 * parent, 2 * one + 1), (2 * parent + 1, 2 * two)]
        return straight, across

    at_first = place(is_first, yhi)
    side1 = side_part(at_first, upper, only1, only1)
    made = down_part(at_first, upper, side1, crown)
    one, two = send_both(made, *family(3, 1, 5))
    above = one + two
    above = above + other_core(above)
    across = lax.ppermute(after(only1, made), "yhi", [(0, 1), (1, 0)])
    left1 = jnp.where(yhi == 0, across, only1)
    right1 = jnp.where(yhi == 0, only1, across)
    root = up_rows(place(is_first), upper, left1, right1)
    root = join_cores(root, core, 0)
    made = down_part(place(is_second, yhi), upper, side2, above)

    fa, fb = family(1, 0, 2), family(5, 4, 6)
    one, two = send_both(
        jnp.where(is_first, root, made),
        fa[0] + fb[0] + [(6, 14), (7, 15)],
        fa[1] + fb[1] + [(6, 2), (7, 3)],
    )
    one, two, *sides = lax.optimization_barrier((one, two, *sides))
    root = jnp.where(group == 7, one, jnp.where(group == 1, two, root))
    above = one + two
    above = above + other_core(above)
    made = down_part(place(is_third, yhi), upper, side3, above, True)
    straight = [(1, 3), (5, 7), (9, 11), (13, 15), (0, 1), (4, 5), (8, 9), (12, 13)]
    across = [(1, 2), (5, 6), (9, 10), (13, 14)]
    straight += [(2, 0), (3, 4), (6, 8), (14, 12), (15, 10)]
    across += [(2, 1), (3, 5), (6, 9), (14, 13), (15, 11)]
    one, two = send_both(jnp.where(is_third, made, root), straight, across)
    has_root = (group == 1) | (group == 3) | (group == 7)
    root = jnp.where(has_root, root, jnp.where(yhi == 0, one, two))
    kept = jnp.where(is_third, made, two)
    last = jnp.where(yhi == 0, kept, one)
    last = last + other_core(last)
    leaf = leaf_rows(whole, sides, last).reshape(2, 4, rows, width)
    leaf = jnp.moveaxis(leaf, 1, 0).reshape(4, 2 * rows, width)
    whole_root = jnp.broadcast_to(root, (4, width, width))
    ends = lax.all_to_all(jnp.concatenate([whole_root, leaf], 1), "x", 0, 0, tiled=True)
    leaf_down = ends[:3, width:].reshape(1, 3, 2, rows, width)
    return leaf_down, ends[:3, :width]


def solution(mesh):
    shape = (2, 2, 2, 2, 4, 2)
    fine = Mesh(mesh.devices.reshape(shape), NODE + BOND)
    placed = (
        P(NODE, BOND, None, None),
        P(None, BOND, NODE, None),
        P(NODE, None, None, None, None),
        P(),
        P(),
    )
    return jax.shard_map(
        local,
        mesh=fine,
        in_specs=placed,
        out_specs=(P(NODE, None, None, BOND, None), P()),
        check_vma=False,
    )
```

```python
import functools

import jax
import jax.numpy as jnp
from jax import lax
from jax.experimental import pallas as pl
from jax.experimental.pallas import tpu as pltpu
from jax.sharding import Mesh, PartitionSpec as P

BF = jnp.bfloat16
F32 = jnp.float32
CHUNKS = 8


def split(v):
    hi = v.astype(BF)
    return hi, (v - hi.astype(F32)).astype(BF)


def wide(v):
    return jnp.concatenate(split(v), axis=1)


def stacked(v):
    row = wide(v)
    return jnp.concatenate([row, row], axis=0)


def mm(a, b):
    return jnp.dot(a, b, preferred_element_type=F32)


def mm_t(a, b):
    return lax.dot_general(a, b, (((1,), (1,)), ((), ())), preferred_element_type=F32)


def fold(v):
    half = v.shape[1] // 2
    return v[:, :half] + v[:, half:]


def product(a_wide, b_stacked):
    return fold(mm(a_wide, b_stacked))


def pair_rows(one, two):
    h1, l1 = split(one)
    h2, l2 = split(two)
    return jnp.concatenate([jnp.concatenate([h1, h2], 1), jnp.concatenate([l1, l2], 1)], 0)


def quarters(acc):
    r = acc.shape[0] // 2
    c = acc.shape[1] // 2
    return (acc[:r, :c] + acc[r:, :c]) + (acc[:r, c:] + acc[r:, c:])


def aligned(i, n):
    return pl.multiple_of(i * n, n)


def chunks_of(src, dst, sems):
    size = dst.shape[0] // CHUNKS

    def copy(i):
        there = pl.ds(aligned(i, size), size)
        return pltpu.make_async_copy(src.at[there], dst.at[there], sems.at[i])

    return copy


def up_kernel(D, H, place_ref, x_ref, l_ref, r_ref, out_ref, n_scr):
    @pl.when(place_ref[2] == 0)
    def _():
        out_ref[...] = jnp.zeros_like(out_ref)

    @pl.when(place_ref[2] == 1)
    def _():
        start = place_ref[0] * H
        rr = stacked(r_ref[...])
        ll = wide(l_ref[...].T)

        def slab(p, carry):
            t = product(wide(x_ref[pl.ds(aligned(start + p, D), D), :]), rr)
            n_scr[pl.ds(p, D, stride=H), :] = product(ll, stacked(t))
            return carry

        lax.fori_loop(0, H, slab, 0, unroll=8)

        def gram(i, acc):
            c = 2 * i
            lhs = pair_rows(n_scr[pl.ds(aligned(c, H), H), :], n_scr[pl.ds(aligned(c + 1, H), H), :])
            rhs = pair_rows(x_ref[pl.ds(c, D, stride=D), :], x_ref[pl.ds(c + 1, D, stride=D), :])
            return acc + mm_t(lhs, rhs)

        acc = lax.fori_loop(0, D // 2, gram, jnp.zeros((2 * H, 2 * D), F32), unroll=8)
        out_ref[...] = quarters(acc)


def side_kernel(D, H, place_ref, x_ref, l_ref, r_ref, s_hbm, s_ref, sem):
    @pl.when((place_ref[2] == 1) & (place_ref[1] == 0))
    def _():
        rr = stacked(r_ref[...])

        def slab(p, carry):
            x = x_ref[pl.ds(aligned(2 * p + place_ref[0], H), H), :]
            s_ref[pl.ds(p, H, stride=D), :] = product(wide(x), rr)
            return carry

        lax.fori_loop(0, D, slab, 0, unroll=8)

    @pl.when((place_ref[2] == 1) & (place_ref[1] == 1))
    def _():
        ll = wide(l_ref[...].T)
        half = jnp.where(place_ref[0] == 0, ll[:H], ll[H:])

        def slab(p, carry):
            x = x_ref[pl.ds(aligned(p, D), D), :]
            s_ref[pl.ds(p, H, stride=D), :] = product(half, stacked(x))
            return carry

        lax.fori_loop(0, D, slab, 0, unroll=8)

    @pl.when(place_ref[2] == 1)
    def _():
        done = pltpu.make_async_copy(s_ref, s_hbm, sem)
        done.start()
        done.wait()


def down_kernel(D, H, stream, place_ref, x_ref, s_hbm, e_ref, out_ref, n_scr, s_ref, s_sems, *own):
    out_ref[...] = jnp.zeros_like(out_ref)
    s_copy = chunks_of(s_hbm, s_ref, s_sems)
    if stream:
        x_hbm = x_ref
        x_ref, x_sems = own
        x_copy = chunks_of(x_hbm, x_ref, x_sems)

    @pl.when(place_ref[2] == 1)
    def _():
        for i in range(CHUNKS):
            s_copy(i).start()
        if stream:
            for i in range(CHUNKS):
                x_copy(i).start()
        start = place_ref[0] * H
        ee = wide(e_ref[...].T)
        per = H // CHUNKS

        def chunk(i, carry):
            s_copy(i).wait()
            for j in range(per):
                v = i * per + j
                t = s_ref[pl.ds(aligned(v, D), D), :]
                n_scr[pl.ds(v, D, stride=H), :] = product(ee, stacked(t))
            return carry

        lax.fori_loop(0, CHUNKS, chunk, 0)
        if stream:
            for i in range(CHUNKS):
                x_copy(i).wait()

        @pl.when(place_ref[1] == 0)
        def _():
            def gram(i, acc):
                q = 2 * i
                lhs = pair_rows(n_scr[pl.ds(aligned(q, H), H), :], n_scr[pl.ds(aligned(q + 1, H), H), :])
                rhs = pair_rows(x_ref[pl.ds(aligned(q, D), D), :], x_ref[pl.ds(aligned(q + 1, D), D), :])
                return acc + mm_t(lhs, rhs)

            acc = lax.fori_loop(0, D // 2, gram, jnp.zeros((2 * H, 2 * D), F32), unroll=8)
            out_ref[pl.ds(aligned(place_ref[0], H), H), :] = quarters(acc)

        @pl.when(place_ref[1] == 1)
        def _():
            def gram(i, acc):
                q = 4 * i
                v = n_scr[pl.ds(aligned(i, 4 * H), 4 * H), :].T
                lhs = jnp.concatenate(split(v), 0)
                x = [x_ref[pl.ds(pl.multiple_of((q + j) * D + start, H), H), :] for j in range(4)]
                return acc + mm(lhs, wide(jnp.concatenate(x, 0)))

            acc = lax.fori_loop(0, D // 4, gram, jnp.zeros((2 * D, 2 * D), F32), unroll=4)
            out_ref[...] = quarters(acc)


def leaf_side_kernel(D, W, K, at_ref, x_hbm, xa_ref, l_ref, r_ref, t_ref, u_ref, x_ref, b_scr, sems):
    copy = chunks_of(x_hbm, x_ref, sems)
    for i in range(CHUNKS):
        copy(i).start()
    for k in range(K):
        rr = stacked(r_ref[k])
        for a in range(W):
            x = xa_ref[pl.ds(a, D, stride=W), :]
            t_ref[pl.ds((k * W + a) * D, D), :] = product(wide(x), rr)
    lane = lax.broadcasted_iota(jnp.int32, (W, D), 1)
    line = lax.broadcasted_iota(jnp.int32, (W, D), 0)
    pick = jnp.where(lane == line + at_ref[0] * W, 1.0, 0.0).astype(BF)
    per = D // CHUNKS

    def chunk(i, carry):
        copy(i).wait()
        for j in range(per):
            p = i * per + j
            x = x_ref[pl.ds(aligned(p, D), D), :]
            b_scr[pl.ds(p, W, stride=D), :] = fold(mm_t(pick, jnp.concatenate(split(x), 0)))
        return carry

    lax.fori_loop(0, CHUNKS, chunk, 0)
    for k in range(K):
        ll = stacked(l_ref[k])
        for b in range(W):
            u_ref[pl.ds((k * W + b) * D, D), :] = product(wide(b_scr[pl.ds(b * D, D), :]), ll)


def leaf_kernel(D, W, K, x_hbm, t_ref, u_ref, e_ref, out_ref, x_ref, n_scr, v_scr, sems):
    copy = chunks_of(x_hbm, x_ref, sems)
    for i in range(CHUNKS):
        copy(i).start()
    R = K * W
    for k in range(K):
        ee = wide(e_ref[k].T)
        for w in range(W):
            r = k * W + w
            n_scr[pl.ds(r, D, stride=R), :] = product(ee, stacked(t_ref[pl.ds(r * D, D), :]))
            v_scr[pl.ds(r, D, stride=R), :] = product(ee, stacked(u_ref[pl.ds(r * D, D), :]))
    for i in range(CHUNKS):
        copy(i).wait()

    def gram(i, accs):
        q = 2 * i
        one, two = pl.ds(aligned(q, R), R), pl.ds(aligned(q + 1, R), R)
        h1, l1 = split(x_ref[pl.ds(aligned(q, D), D), :])
        h2, l2 = split(x_ref[pl.ds(aligned(q + 1, D), D), :])
        cat = jnp.concatenate
        by_last = cat([cat([h1, h2], 1), cat([l1, l2], 1)], 0)
        by_first = cat([cat([h1, l1], 1), cat([h2, l2], 1)], 0)
        first = mm_t(pair_rows(n_scr[one, :], n_scr[two, :]), by_last)
        second = mm(pair_rows(v_scr[one, :], v_scr[two, :]), by_first)
        return accs[0] + first, accs[1] + second

    zero = jnp.zeros((2 * R, 2 * D), F32)
    first, second = lax.fori_loop(0, D // 2, gram, (zero, zero), unroll=4)
    first = quarters(first)
    second = quarters(second)
    for k in range(K):
        out_ref[k, 0] = first[k * W : (k + 1) * W]
        out_ref[k, 1] = second[k * W : (k + 1) * W]


VMEM = pl.BlockSpec(memory_space=pltpu.VMEM)
HBM = pl.BlockSpec(memory_space=pltpu.HBM)
SMEM = pl.BlockSpec(memory_space=pltpu.SMEM)


def call(kernel, name, mib, units, out_shape, in_specs, out_specs, scratch):
    return pl.pallas_call(
        kernel,
        out_shape=out_shape,
        in_specs=in_specs,
        out_specs=out_specs,
        scratch_shapes=scratch,
        compiler_params=pltpu.CompilerParams(vmem_limit_bytes=mib << 20),
        cost_estimate=pl.CostEstimate(
            flops=int(units * 4.8e9), bytes_accessed=8 << 20, transcendentals=0
        ),
        name=name,
    )


def up_rows(place, tensor, left_env, right_env, cuts=2):
    D = left_env.shape[0]
    H = D // cuts
    return call(
        functools.partial(up_kernel, D, H),
        "up",
        44,
        1,
        jax.ShapeDtypeStruct((H, D), F32),
        [SMEM, VMEM, VMEM, VMEM],
        VMEM,
        [pltpu.VMEM((D * H, D), F32)],
    )(place, tensor.reshape(D * D, D), left_env, right_env)


def side_part(place, tensor, left_env, right_env):
    D = left_env.shape[0]
    H = D // 2
    return call(
        functools.partial(side_kernel, D, H),
        "side",
        53,
        0.4,
        jax.ShapeDtypeStruct((D * H, D), F32),
        [SMEM, VMEM, VMEM, VMEM],
        HBM,
        [pltpu.VMEM((D * H, D), F32), pltpu.SemaphoreType.DMA],
    )(place, tensor.reshape(D * D, D), left_env, right_env)


def down_part(place, tensor, side, above, stream=False):
    D = above.shape[0]
    H = D // 2
    half = pltpu.VMEM((D * H, D), F32)
    sems = pltpu.SemaphoreType.DMA((CHUNKS,))
    return call(
        functools.partial(down_kernel, D, H, stream),
        "down",
        57 if stream else 53,
        0.7,
        jax.ShapeDtypeStruct((D, D), F32),
        [SMEM, HBM if stream else VMEM, HBM, VMEM],
        VMEM,
        [half, half, sems] + ([pltpu.VMEM((D * D, D), F32), sems] if stream else []),
    )(place, tensor.reshape(D * D, D), side, above)


def leaf_sides(at, whole, slab, left, right):
    K, D = left.shape[:2]
    W = slab.shape[1]
    rows = jax.ShapeDtypeStruct((K * W * D, D), F32)
    return call(
        functools.partial(leaf_side_kernel, D, W, K),
        "leaf_side",
        57,
        0.7,
        (rows, rows),
        [SMEM, HBM, VMEM, VMEM, VMEM],
        (VMEM, VMEM),
        [pltpu.VMEM((D * D, D), F32), pltpu.VMEM((W * D, D), F32), pltpu.SemaphoreType.DMA((CHUNKS,))],
    )(at.reshape(1), whole.reshape(D * D, D), slab.reshape(D * W, D), left, right)


def leaf_rows(whole, sides, above):
    K, D = above.shape[:2]
    W = sides[0].shape[0] // (K * D)
    rows = pltpu.VMEM((K * W * D, D), F32)
    return call(
        functools.partial(leaf_kernel, D, W, K),
        "leaf",
        57,
        0.7,
        jax.ShapeDtypeStruct((K, 2, W, D), F32),
        [HBM, VMEM, VMEM, VMEM],
        VMEM,
        [pltpu.VMEM((D * D, D), F32), rows, rows, pltpu.SemaphoreType.DMA((CHUNKS,))],
    )(whole.reshape(D * D, D), sides[0], sides[1], above)


NODE = ("ylo", "zhi", "zlo")
BOND = ("yhi", "x", "core")
SLOT_OF = (4, 2, 5, 1, 6, 3, 7, 0)


def ein(spec, a, b):
    return jnp.einsum(spec, a, b, precision=lax.Precision.HIGHEST)


def after(x, other):
    return lax.optimization_barrier((x, other))[0]


def other_core(x):
    return lax.ppermute(x, "core", [(0, 1), (1, 0)])


def join_cores(half, core, axis):
    other = other_core(half)
    low = jnp.where(core == 0, half, other)
    high = jnp.where(core == 0, other, half)
    return jnp.concatenate([low, high], axis=axis)


def reorder_kernel(in_ref, out_ref):
    for g, s in enumerate(SLOT_OF):
        out_ref[g] = in_ref[s]


def reordered(x):
    return pl.pallas_call(
        reorder_kernel,
        out_shape=jax.ShapeDtypeStruct(x.shape, x.dtype),
        in_specs=[VMEM],
        out_specs=VMEM,
        compiler_params=pltpu.CompilerParams(vmem_limit_bytes=8 << 20),
        name="reorder",
    )(x)


def local(bottom_nodes, upper_nodes, leaf_up, outside_env, top_env):
    group = lax.axis_index(NODE)
    bond = lax.axis_index(BOND)
    core = lax.axis_index("core")
    yhi = lax.axis_index("yhi")
    op = jnp.minimum(lax.axis_index("x"), 2)
    width = bottom_nodes.shape[2]
    rows = bottom_nodes.shape[1]
    parts = width // rows

    got = lax.all_to_all(reordered(upper_nodes), NODE, 0, 0, tiled=True)
    shard = jnp.moveaxis(got, 0, 1).reshape(rows, width, width)
    upper = lax.all_gather(shard, BOND, axis=0, tiled=True)

    mine = bottom_nodes[0]
    left_leaf = leaf_up[0, :, 0]
    right_leaf = leaf_up[0, :, 1]
    middle = ein("kac,pcd->kpad", left_leaf, after(mine, shard))
    product = ein("kpad,kbd->kpab", middle, right_leaf)
    both = jnp.concatenate([mine[None], product])
    both = jnp.moveaxis(both.reshape(4, rows, parts, rows, width), 2, 0)
    both = lax.all_to_all(both, BOND, 0, 0, tiled=True)
    both = jnp.moveaxis(both, 1, 0).reshape(4, width, rows, width)
    mine_a = both[0]
    gram = ein("pab,kqab->kpq", mine_a, both[1:])
    pieces = jnp.moveaxis(gram.reshape(3, parts, rows, width), 1, 0)
    pieces = lax.all_to_all(pieces, BOND, 0, 0, tiled=True)
    env = jnp.sum(pieces, axis=0)
    by_x = jnp.stack([env[0], env[1], env[2], env[2]])
    by_dest = jnp.broadcast_to(by_x[None, None, :, None], (2, 2, 4, 2, rows, width))
    by_dest = by_dest.reshape(2 * parts, rows, width)
    pair = lax.all_to_all(by_dest, ("zlo",) + BOND, 0, 0, tiled=True)
    left3, right3 = pair.reshape(2, width, width)

    def move(x, *pairs):
        return lax.ppermute(x, NODE, pairs)

    def place(active, which=jnp.int32(0)):
        return jnp.stack([core, which, active.astype(jnp.int32)])

    is_third = group % 2 == 0
    is_second = (group == 1) | (group == 5)
    is_first = group == 3

    whole = lax.all_gather(after(mine, left3), BOND, axis=0, tiled=True)
    sides = leaf_sides(bond, whole, mine_a, left_leaf, right_leaf)

    up2 = up_rows(place(is_third), upper, left3, right3)
    ends = jnp.stack([move(up2, (0, 1), (4, 5)), move(up2, (2, 1), (6, 5))])
    left2, right2 = join_cores(ends, core, 1)
    top = lax.dynamic_index_in_dim(top_env, op, 0, keepdims=False)
    outside = lax.dynamic_index_in_dim(outside_env, op, 0, keepdims=False)
    at_crown = place(group == 7)
    crown = down_part(at_crown, upper, side_part(at_crown, upper, outside, outside), top)
    crown = move(crown, (7, 3))
    crown = crown + other_core(crown)
    side3 = side_part(place(is_third, yhi), upper, left3, right3)
    left2, right2, side3 = lax.optimization_barrier((left2, right2, side3))
    up1 = up_rows(place(is_second), upper, left2, right2)
    ends = jnp.stack([move(up1, (1, 3)), move(up1, (5, 3))])
    left1, right1 = join_cores(ends, core, 1)
    side2 = side_part(place(is_second, yhi), upper, left2, right2)
    left1, right1, side2 = lax.optimization_barrier((left1, right1, side2))

    def send_both(x, straight, across):
        axes = NODE + ("yhi",)
        return lax.ppermute(x, axes, straight), lax.ppermute(x, axes, across)

    def family(parent, one, two):
        straight = [(2 * parent, 2 * one), (2 * parent + 1, 2 * two + 1)]
        across = [(2 * parent, 2 * one + 1), (2 * parent + 1, 2 * two)]
        return straight, across

    at_first = place(is_first, yhi)
    side1 = side_part(at_first, upper, left1, right1)
    made = down_part(at_first, upper, side1, crown)
    one, two = send_both(made, *family(3, 1, 5))
    above = one + two
    above = above + other_core(above)
    root = up_rows(place(is_first), upper, left1, after(right1, made))
    root = join_cores(root, core, 0)
    made = down_part(place(is_second, yhi), upper, side2, above)

    fa, fb = family(1, 0, 2), family(5, 4, 6)
    one, two = send_both(
        jnp.where(is_first, root, made),
        fa[0] + fb[0] + [(6, 14), (7, 15)],
        fa[1] + fb[1] + [(6, 2), (7, 3)],
    )
    one, two, *sides = lax.optimization_barrier((one, two, *sides))
    root = jnp.where(group == 7, one, jnp.where(group == 1, two, root))
    above = one + two
    above = above + other_core(above)
    made = down_part(place(is_third, yhi), upper, side3, above, True)
    straight = [(1, 3), (5, 7), (9, 11), (13, 15), (0, 1), (4, 5), (8, 9), (12, 13)]
    across = [(1, 2), (5, 6), (9, 10), (13, 14)]
    straight += [(2, 0), (3, 4), (6, 8), (14, 12), (15, 10)]
    across += [(2, 1), (3, 5), (6, 9), (14, 13), (15, 11)]
    one, two = send_both(jnp.where(is_third, made, root), straight, across)
    has_root = (group == 1) | (group == 3) | (group == 7)
    root = jnp.where(has_root, root, jnp.where(yhi == 0, one, two))
    kept = jnp.where(is_third, made, two)
    last = jnp.where(yhi == 0, kept, one)
    last = last + other_core(last)
    ends = lax.all_gather(jnp.stack([last, root]), "x", axis=0, tiled=False)
    above = ends[:3, 0]
    root_env = ends[:3, 1]
    return leaf_rows(whole, sides, above)[None], root_env


def solution(mesh):
    shape = (2, 2, 2, 2, 4, 2)
    fine = Mesh(mesh.devices.reshape(shape), NODE + BOND)
    placed = (
        P(NODE, BOND, None, None),
        P(None, BOND, NODE, None),
        P(NODE, None, None, None, None),
        P(),
        P(),
    )
    return jax.shard_map(
        local,
        mesh=fine,
        in_specs=placed,
        out_specs=(P(NODE, None, None, BOND, None), P()),
        check_vma=False,
    )
```

```python
import functools

import jax
import jax.numpy as jnp
from jax import lax
from jax.experimental import pallas as pl
from jax.experimental.pallas import tpu as pltpu
from jax.sharding import Mesh, PartitionSpec as P

BF = jnp.bfloat16
F32 = jnp.float32
CHUNKS = 8


def split(v):
    hi = v.astype(BF)
    return hi, (v - hi.astype(F32)).astype(BF)


def wide(v):
    return jnp.concatenate(split(v), axis=1)


def stacked(v):
    row = wide(v)
    return jnp.concatenate([row, row], axis=0)


def mm(a, b):
    return jnp.dot(a, b, preferred_element_type=F32)


def mm_t(a, b):
    return lax.dot_general(a, b, (((1,), (1,)), ((), ())), preferred_element_type=F32)


def fold(v):
    half = v.shape[1] // 2
    return v[:, :half] + v[:, half:]


def product(a_wide, b_stacked):
    return fold(mm(a_wide, b_stacked))


def pair_rows(one, two):
    h1, l1 = split(one)
    h2, l2 = split(two)
    return jnp.concatenate([jnp.concatenate([h1, h2], 1), jnp.concatenate([l1, l2], 1)], 0)


def quarters(acc):
    r = acc.shape[0] // 2
    c = acc.shape[1] // 2
    return (acc[:r, :c] + acc[r:, :c]) + (acc[:r, c:] + acc[r:, c:])


def aligned(i, n):
    return pl.multiple_of(i * n, n)


def fetch(src, dst, sems, count, first=0):
    size = dst.shape[0] // count

    def copy(i):
        at = lax.rem(first + i, count)
        there = pl.ds(aligned(at, size), size)
        return pltpu.make_async_copy(src.at[there], dst.at[there], sems.at[i])

    return copy


def up_kernel(D, H, many, place_ref, x_hbm, l_ref, r_ref, out_ref, x_ref, n_scr, sems):
    @pl.when(place_ref[2] == 0)
    def _():
        out_ref[...] = jnp.zeros_like(out_ref)

    @pl.when(place_ref[2] == 1)
    def _():
        count = 2 * CHUNKS
        copy = fetch(x_hbm, x_ref, sems, count, place_ref[0] * CHUNKS)
        for i in range(count):
            copy(i).start()
        start = place_ref[0] * H
        rr = stacked(r_ref[...])
        ll = wide(l_ref[...].T)
        per = 2 * H // CHUNKS

        def chunk(i, carry):
            copy(2 * i).wait()
            copy(2 * i + 1).wait()
            def one(j, carry):
                p = i * per + j
                t = product(wide(x_ref[pl.ds(aligned(start + p, D), D), :]), rr)
                n_scr[pl.ds(p, D, stride=H), :] = product(ll, stacked(t))
                return carry

            lax.fori_loop(0, per, one, 0, unroll=min(many, per))
            return carry

        lax.fori_loop(0, CHUNKS // 2, chunk, 0)
        for i in range(CHUNKS, count):
            copy(i).wait()

        def gram(i, acc):
            c = 2 * i
            lhs = pair_rows(n_scr[pl.ds(aligned(c, H), H), :], n_scr[pl.ds(aligned(c + 1, H), H), :])
            rhs = pair_rows(x_ref[pl.ds(c, D, stride=D), :], x_ref[pl.ds(c + 1, D, stride=D), :])
            return acc + mm_t(lhs, rhs)

        acc = lax.fori_loop(0, D // 2, gram, jnp.zeros((2 * H, 2 * D), F32), unroll=many)
        out_ref[...] = quarters(acc)


def side_kernel(D, H, many, place_ref, x_hbm, l_ref, r_ref, s_hbm, x_ref, s_ref, sems):
    @pl.when(place_ref[2] == 1)
    def _():
        copy = fetch(x_hbm, x_ref, sems, CHUNKS)
        for i in range(CHUNKS):
            copy(i).start()
        start = place_ref[0] * H
        per = D // CHUNKS

        @pl.when(place_ref[1] == 0)
        def _():
            rr = stacked(r_ref[...])

            def chunk(i, carry):
                copy(i).wait()
                def one(j, carry):
                    p = i * per + j
                    x = x_ref[pl.ds(aligned(2 * p + place_ref[0], H), H), :]
                    s_ref[pl.ds(p, H, stride=D), :] = product(wide(x), rr)
                    return carry

                lax.fori_loop(0, per, one, 0, unroll=min(many, per))
                return carry

            lax.fori_loop(0, CHUNKS, chunk, 0)

        @pl.when(place_ref[1] == 1)
        def _():
            ll = wide(l_ref[...].T)
            half = jnp.where(place_ref[0] == 0, ll[:H], ll[H:])

            def chunk(i, carry):
                copy(i).wait()
                def one(j, carry):
                    p = i * per + j
                    x = x_ref[pl.ds(aligned(p, D), D), :]
                    s_ref[pl.ds(p, H, stride=D), :] = product(half, stacked(x))
                    return carry

                lax.fori_loop(0, per, one, 0, unroll=min(many, per))
                return carry

            lax.fori_loop(0, CHUNKS, chunk, 0)

        done = pltpu.make_async_copy(s_ref, s_hbm, sems.at[0])
        done.start()
        done.wait()


def down_kernel(D, H, many, place_ref, x_hbm, s_hbm, e_ref, out_ref, x_ref, s_ref, n_scr, sems):
    out_ref[...] = jnp.zeros_like(out_ref)

    @pl.when(place_ref[2] == 1)
    def _():
        s_copy = fetch(s_hbm, s_ref, sems, CHUNKS)
        x_copy = fetch(x_hbm, x_ref, sems.at[pl.ds(CHUNKS, CHUNKS)], CHUNKS)
        for i in range(CHUNKS):
            s_copy(i).start()
        for i in range(CHUNKS):
            x_copy(i).start()
        start = place_ref[0] * H
        ee = wide(e_ref[...].T)
        per = 2 * H // CHUNKS

        def chunk(i, carry):
            s_copy(2 * i).wait()
            s_copy(2 * i + 1).wait()
            def one(j, carry):
                v = i * per + j
                t = s_ref[pl.ds(aligned(v, D), D), :]
                n_scr[pl.ds(v, D, stride=H), :] = product(ee, stacked(t))
                return carry

            lax.fori_loop(0, per, one, 0, unroll=min(many, per))
            return carry

        lax.fori_loop(0, CHUNKS // 2, chunk, 0)
        for i in range(CHUNKS):
            x_copy(i).wait()

        @pl.when(place_ref[1] == 0)
        def _():
            def gram(i, acc):
                q = 2 * i
                lhs = pair_rows(n_scr[pl.ds(aligned(q, H), H), :], n_scr[pl.ds(aligned(q + 1, H), H), :])
                rhs = pair_rows(x_ref[pl.ds(aligned(q, D), D), :], x_ref[pl.ds(aligned(q + 1, D), D), :])
                return acc + mm_t(lhs, rhs)

            acc = lax.fori_loop(0, D // 2, gram, jnp.zeros((2 * H, 2 * D), F32), unroll=many)
            out_ref[pl.ds(aligned(place_ref[0], H), H), :] = quarters(acc)

        @pl.when(place_ref[1] == 1)
        def _():
            def gram(i, acc):
                q = 4 * i
                v = n_scr[pl.ds(aligned(i, 4 * H), 4 * H), :].T
                lhs = jnp.concatenate(split(v), 0)
                x = [x_ref[pl.ds(pl.multiple_of((q + j) * D + start, H), H), :] for j in range(4)]
                return acc + mm(lhs, wide(jnp.concatenate(x, 0)))

            acc = lax.fori_loop(0, D // 4, gram, jnp.zeros((2 * D, 2 * D), F32), unroll=many // 2)
            out_ref[...] = quarters(acc)


def leaf_side_kernel(D, W, K, at_ref, x_hbm, xa_ref, l_ref, r_ref, t_ref, u_ref, x_ref, b_scr, sems):
    copy = fetch(x_hbm, x_ref, sems, CHUNKS)
    for i in range(CHUNKS):
        copy(i).start()
    def right(k, carry):
        rr = stacked(r_ref[k])
        for a in range(W):
            x = xa_ref[pl.ds(a, D, stride=W), :]
            t_ref[pl.ds(aligned(k * W + a, D), D), :] = product(wide(x), rr)
        return carry

    lax.fori_loop(0, K, right, 0)
    lane = lax.broadcasted_iota(jnp.int32, (W, D), 1)
    line = lax.broadcasted_iota(jnp.int32, (W, D), 0)
    pick = jnp.where(lane == line + at_ref[0] * W, 1.0, 0.0).astype(BF)
    per = D // CHUNKS

    def chunk(i, carry):
        copy(i).wait()
        for j in range(per):
            p = i * per + j
            x = x_ref[pl.ds(aligned(p, D), D), :]
            b_scr[pl.ds(p, W, stride=D), :] = fold(mm_t(pick, jnp.concatenate(split(x), 0)))
        return carry

    lax.fori_loop(0, CHUNKS, chunk, 0)

    def left(k, carry):
        ll = stacked(l_ref[k])
        for b in range(W):
            u_ref[pl.ds(aligned(k * W + b, D), D), :] = product(wide(b_scr[pl.ds(b * D, D), :]), ll)
        return carry

    lax.fori_loop(0, K, left, 0)


def leaf_kernel(D, W, K, x_hbm, t_ref, u_ref, e_ref, out_ref, x_ref, n_scr, v_scr, sems):
    copy = fetch(x_hbm, x_ref, sems, CHUNKS)
    for i in range(CHUNKS):
        copy(i).start()
    R = K * W

    def mix(k, carry):
        ee = wide(e_ref[k].T)
        for w in range(W):
            r = k * W + w
            at = pl.ds(aligned(r, D), D)
            n_scr[pl.ds(r, D, stride=R), :] = product(ee, stacked(t_ref[at, :]))
            v_scr[pl.ds(r, D, stride=R), :] = product(ee, stacked(u_ref[at, :]))
        return carry

    lax.fori_loop(0, K, mix, 0)
    for i in range(CHUNKS):
        copy(i).wait()

    def gram(i, accs):
        q = 2 * i
        one, two = pl.ds(aligned(q, R), R), pl.ds(aligned(q + 1, R), R)
        h1, l1 = split(x_ref[pl.ds(aligned(q, D), D), :])
        h2, l2 = split(x_ref[pl.ds(aligned(q + 1, D), D), :])
        cat = jnp.concatenate
        by_last = cat([cat([h1, h2], 1), cat([l1, l2], 1)], 0)
        by_first = cat([cat([h1, l1], 1), cat([h2, l2], 1)], 0)
        first = mm_t(pair_rows(n_scr[one, :], n_scr[two, :]), by_last)
        second = mm(pair_rows(v_scr[one, :], v_scr[two, :]), by_first)
        return accs[0] + first, accs[1] + second

    zero = jnp.zeros((2 * R, 2 * D), F32)
    first, second = lax.fori_loop(0, D // 2, gram, (zero, zero), unroll=4)
    first = quarters(first)
    second = quarters(second)
    for k in range(K):
        out_ref[k, 0] = first[k * W : (k + 1) * W]
        out_ref[k, 1] = second[k * W : (k + 1) * W]


VMEM = pl.BlockSpec(memory_space=pltpu.VMEM)
SMEM = pl.BlockSpec(memory_space=pltpu.SMEM)
HBM = pl.BlockSpec(memory_space=pltpu.HBM)


def call(kernel, name, mib, units, out_shape, in_specs, out_specs, scratch):
    return pl.pallas_call(
        kernel,
        out_shape=out_shape,
        in_specs=in_specs,
        out_specs=out_specs,
        scratch_shapes=scratch,
        compiler_params=pltpu.CompilerParams(vmem_limit_bytes=mib << 20),
        cost_estimate=pl.CostEstimate(
            flops=int(units * 4.8e9), bytes_accessed=8 << 20, transcendentals=0
        ),
        name=name,
    )


def up_rows(place, tensor, left_env, right_env, many=16):
    D = left_env.shape[0]
    H = D // 2
    return call(
        functools.partial(up_kernel, D, H, many),
        "up",
        57,
        1,
        jax.ShapeDtypeStruct((H, D), F32),
        [SMEM, HBM, VMEM, VMEM],
        VMEM,
        [pltpu.VMEM((D * D, D), F32), pltpu.VMEM((D * H, D), F32), pltpu.SemaphoreType.DMA((2 * CHUNKS,))],
    )(place, tensor.reshape(D * D, D), left_env, right_env)


def side_part(place, tensor, left_env, right_env, many=8):
    D = left_env.shape[0]
    H = D // 2
    return call(
        functools.partial(side_kernel, D, H, many),
        "side",
        57,
        0.4,
        jax.ShapeDtypeStruct((D * H, D), F32),
        [SMEM, HBM, VMEM, VMEM],
        HBM,
        [pltpu.VMEM((D * D, D), F32), pltpu.VMEM((D * H, D), F32), pltpu.SemaphoreType.DMA((CHUNKS,))],
    )(place, tensor.reshape(D * D, D), left_env, right_env)


def down_part(place, tensor, side, above, many=16):
    D = above.shape[0]
    H = D // 2
    big = pltpu.VMEM((D * D, D), F32)
    half = pltpu.VMEM((D * H, D), F32)
    return call(
        functools.partial(down_kernel, D, H, many),
        "down",
        57,
        0.7,
        jax.ShapeDtypeStruct((D, D), F32),
        [SMEM, HBM, HBM, VMEM],
        VMEM,
        [big, half, half, pltpu.SemaphoreType.DMA((2 * CHUNKS,))],
    )(place, tensor.reshape(D * D, D), side, above)


def leaf_sides(at, whole, slab, left, right):
    K, D = left.shape[:2]
    W = slab.shape[1]
    rows = jax.ShapeDtypeStruct((K * W * D, D), F32)
    return call(
        functools.partial(leaf_side_kernel, D, W, K),
        "leaf_side",
        57,
        0.7,
        (rows, rows),
        [SMEM, HBM, VMEM, VMEM, VMEM],
        (VMEM, VMEM),
        [pltpu.VMEM((D * D, D), F32), pltpu.VMEM((W * D, D), F32), pltpu.SemaphoreType.DMA((CHUNKS,))],
    )(at.reshape(1), whole.reshape(D * D, D), slab.reshape(D * W, D), left, right)


def leaf_rows(whole, sides, above):
    K, D = above.shape[:2]
    W = sides[0].shape[0] // (K * D)
    rows = pltpu.VMEM((K * W * D, D), F32)
    return call(
        functools.partial(leaf_kernel, D, W, K),
        "leaf",
        57,
        0.7,
        jax.ShapeDtypeStruct((K, 2, W, D), F32),
        [HBM, VMEM, VMEM, VMEM],
        VMEM,
        [pltpu.VMEM((D * D, D), F32), rows, rows, pltpu.SemaphoreType.DMA((CHUNKS,))],
    )(whole.reshape(D * D, D), sides[0], sides[1], above)


NODE = ("ylo", "zhi", "zlo")
BOND = ("yhi", "x", "core")
SLOT_OF = (4, 2, 5, 1, 6, 3, 7, 0)


def ein(spec, a, b):
    return jnp.einsum(spec, a, b, precision=lax.Precision.HIGHEST)


def after(x, other):
    return lax.optimization_barrier((x, other))[0]


def other_core(x):
    return lax.ppermute(x, "core", [(0, 1), (1, 0)])


def join_cores(half, core, axis):
    other = other_core(half)
    low = jnp.where(core == 0, half, other)
    high = jnp.where(core == 0, other, half)
    return jnp.concatenate([low, high], axis=axis)


def reorder_kernel(in_ref, out_ref):
    for g, s in enumerate(SLOT_OF):
        out_ref[g] = in_ref[s]


def reordered(x):
    return pl.pallas_call(
        reorder_kernel,
        out_shape=jax.ShapeDtypeStruct(x.shape, x.dtype),
        in_specs=[VMEM],
        out_specs=VMEM,
        compiler_params=pltpu.CompilerParams(vmem_limit_bytes=8 << 20),
        name="reorder",
    )(x)


def local(bottom_nodes, upper_nodes, leaf_up, outside_env, top_env):
    group = lax.axis_index(NODE)
    bond = lax.axis_index(BOND)
    core = lax.axis_index("core")
    yhi = lax.axis_index("yhi")
    op = jnp.minimum(lax.axis_index("x"), 2)
    width = bottom_nodes.shape[2]
    rows = bottom_nodes.shape[1]
    parts = width // rows

    got = lax.all_to_all(reordered(upper_nodes), NODE, 0, 0, tiled=True)
    shard = jnp.moveaxis(got, 0, 1).reshape(rows, width, width)
    upper = lax.all_gather(shard, BOND, axis=0, tiled=True)

    mine = bottom_nodes[0]
    left_leaf = leaf_up[0, :, 0]
    right_leaf = leaf_up[0, :, 1]
    middle = ein("kac,pcd->kpad", left_leaf, after(mine, shard))
    product = ein("kpad,kbd->kpab", middle, right_leaf)
    both = jnp.concatenate([mine[None], product])
    both = jnp.moveaxis(both.reshape(4, rows, parts, rows, width), 2, 0)
    both = lax.all_to_all(both, BOND, 0, 0, tiled=True)
    both = jnp.moveaxis(both, 1, 0).reshape(4, width, rows, width)
    mine_a = both[0]
    gram = ein("pab,kqab->kpq", mine_a, both[1:])
    pieces = jnp.moveaxis(gram.reshape(3, parts, rows, width), 1, 0)
    pieces = lax.all_to_all(pieces, BOND, 0, 0, tiled=True)
    env = jnp.sum(pieces, axis=0)
    by_x = jnp.stack([env[0], env[1], env[2], env[2]])
    by_dest = jnp.broadcast_to(by_x[None, None, :, None], (2, 2, 4, 2, rows, width))
    by_dest = by_dest.reshape(2 * parts, rows, width)
    pair = lax.all_to_all(by_dest, ("zlo",) + BOND, 0, 0, tiled=True)
    left3, right3 = pair.reshape(2, width, width)

    def move(x, *pairs):
        return lax.ppermute(x, NODE, pairs)

    def place(active, which=jnp.int32(0)):
        return jnp.stack([core, which, active.astype(jnp.int32)])

    is_third = group % 2 == 0
    is_second = (group == 1) | (group == 5)
    is_first = group == 3

    whole = lax.all_gather(after(mine, left3), BOND, axis=0, tiled=True)
    sides = leaf_sides(bond, whole, mine_a, left_leaf, right_leaf)

    up2 = up_rows(place(is_third), upper, left3, right3)
    ends = jnp.stack([move(up2, (0, 1), (4, 5)), move(up2, (2, 1), (6, 5))])
    left2, right2 = join_cores(ends, core, 1)
    top = lax.dynamic_index_in_dim(top_env, op, 0, keepdims=False)
    outside = lax.dynamic_index_in_dim(outside_env, op, 0, keepdims=False)
    at_crown = place(group == 7)
    crown = side_part(at_crown, upper, outside, outside, 2)
    crown = down_part(at_crown, upper, crown, top, 2)
    crown = move(crown, (7, 3))
    crown = crown + other_core(crown)
    side3 = side_part(place(is_third, yhi), upper, left3, right3)
    left2, right2, side3 = lax.optimization_barrier((left2, right2, side3))
    up1 = up_rows(place(is_second), upper, left2, right2)
    ends = jnp.stack([move(up1, (1, 3)), move(up1, (5, 3))])
    left1, right1 = join_cores(ends, core, 1)
    side2 = side_part(place(is_second, yhi), upper, left2, right2)
    left1, right1, side2 = lax.optimization_barrier((left1, right1, side2))

    def send_both(x, straight, across):
        axes = NODE + ("yhi",)
        return lax.ppermute(x, axes, straight), lax.ppermute(x, axes, across)

    def family(parent, one, two):
        straight = [(2 * parent, 2 * one), (2 * parent + 1, 2 * two + 1)]
        across = [(2 * parent, 2 * one + 1), (2 * parent + 1, 2 * two)]
        return straight, across

    at_first = place(is_first, yhi)
    side1 = side_part(at_first, upper, left1, right1)
    made = down_part(at_first, upper, side1, crown)
    one, two = send_both(made, *family(3, 1, 5))
    above = one + two
    above = above + other_core(above)
    root = up_rows(place(is_first), upper, left1, after(right1, made), 4)
    root = join_cores(root, core, 0)
    made = down_part(place(is_second, yhi), upper, side2, above)

    fa, fb = family(1, 0, 2), family(5, 4, 6)
    one, two = send_both(
        jnp.where(is_first, root, made),
        fa[0] + fb[0] + [(6, 14), (7, 15)],
        fa[1] + fb[1] + [(6, 2), (7, 3)],
    )
    one, two, *sides = lax.optimization_barrier((one, two, *sides))
    root = jnp.where(group == 7, one, jnp.where(group == 1, two, root))
    above = one + two
    above = above + other_core(above)
    made = down_part(place(is_third, yhi), upper, side3, above)
    straight = [(1, 3), (5, 7), (9, 11), (13, 15), (0, 1), (4, 5), (8, 9), (12, 13)]
    across = [(1, 2), (5, 6), (9, 10), (13, 14)]
    straight += [(2, 0), (3, 4), (6, 8), (14, 12), (15, 10)]
    across += [(2, 1), (3, 5), (6, 9), (14, 13), (15, 11)]
    one, two = send_both(jnp.where(is_third, made, root), straight, across)
    has_root = (group == 1) | (group == 3) | (group == 7)
    root = jnp.where(has_root, root, jnp.where(yhi == 0, one, two))
    kept = jnp.where(is_third, made, two)
    last = jnp.where(yhi == 0, kept, one)
    last = last + other_core(last)
    ends = lax.all_gather(jnp.stack([last, root]), "x", axis=0, tiled=False)
    above = ends[:3, 0]
    root_env = ends[:3, 1]
    return leaf_rows(whole, sides, above)[None], root_env


def solution(mesh):
    shape = (2, 2, 2, 2, 4, 2)
    fine = Mesh(mesh.devices.reshape(shape), NODE + BOND)
    placed = (
        P(NODE, BOND, None, None),
        P(None, BOND, NODE, None),
        P(NODE, None, None, None, None),
        P(),
        P(),
    )
    return jax.shard_map(
        local,
        mesh=fine,
        in_specs=placed,
        out_specs=(P(NODE, None, None, BOND, None), P()),
        check_vma=False,
    )
```

```python
import functools

import jax
import jax.numpy as jnp
from jax import lax
from jax.experimental import pallas as pl
from jax.experimental.pallas import tpu as pltpu
from jax.sharding import Mesh, PartitionSpec as P

BF = jnp.bfloat16
F32 = jnp.float32
CHUNKS = 8


def split(v):
    hi = v.astype(BF)
    return hi, (v - hi.astype(F32)).astype(BF)


def wide(v):
    return jnp.concatenate(split(v), axis=1)


def stacked(v):
    row = wide(v)
    return jnp.concatenate([row, row], axis=0)


def mm(a, b):
    return jnp.dot(a, b, preferred_element_type=F32)


def mm_t(a, b):
    return lax.dot_general(a, b, (((1,), (1,)), ((), ())), preferred_element_type=F32)


def fold(v):
    half = v.shape[1] // 2
    return v[:, :half] + v[:, half:]


def product(a_wide, b_stacked):
    return fold(mm(a_wide, b_stacked))


def pair_rows(one, two):
    h1, l1 = split(one)
    h2, l2 = split(two)
    return jnp.concatenate([jnp.concatenate([h1, h2], 1), jnp.concatenate([l1, l2], 1)], 0)


def quarters(acc):
    r = acc.shape[0] // 2
    c = acc.shape[1] // 2
    return (acc[:r, :c] + acc[r:, :c]) + (acc[:r, c:] + acc[r:, c:])


def aligned(i, n):
    return pl.multiple_of(i * n, n)


def fetch(src, dst, sems, count, first=0):
    size = dst.shape[0] // count

    def copy(i):
        at = lax.rem(first + i, count)
        there = pl.ds(aligned(at, size), size)
        return pltpu.make_async_copy(src.at[there], dst.at[there], sems.at[i])

    return copy


def up_kernel(D, H, many, place_ref, x_hbm, l_ref, r_ref, out_ref, x_ref, n_scr, sems):
    @pl.when(place_ref[2] == 0)
    def _():
        out_ref[...] = jnp.zeros_like(out_ref)

    @pl.when(place_ref[2] == 1)
    def _():
        count = 2 * CHUNKS
        copy = fetch(x_hbm, x_ref, sems, count, place_ref[0] * CHUNKS)
        for i in range(count):
            copy(i).start()
        start = place_ref[0] * H
        rr = stacked(r_ref[...])
        ll = wide(l_ref[...].T)
        per = 2 * H // CHUNKS

        def chunk(i, carry):
            copy(2 * i).wait()
            copy(2 * i + 1).wait()
            def one(j, carry):
                p = i * per + j
                t = product(wide(x_ref[pl.ds(aligned(start + p, D), D), :]), rr)
                n_scr[pl.ds(p, D, stride=H), :] = product(ll, stacked(t))
                return carry

            lax.fori_loop(0, per, one, 0, unroll=min(many, per))
            return carry

        lax.fori_loop(0, CHUNKS // 2, chunk, 0)
        for i in range(CHUNKS, count):
            copy(i).wait()

        def gram(i, acc):
            c = 2 * i
            lhs = pair_rows(n_scr[pl.ds(aligned(c, H), H), :], n_scr[pl.ds(aligned(c + 1, H), H), :])
            rhs = pair_rows(x_ref[pl.ds(c, D, stride=D), :], x_ref[pl.ds(c + 1, D, stride=D), :])
            return acc + mm_t(lhs, rhs)

        acc = lax.fori_loop(0, D // 2, gram, jnp.zeros((2 * H, 2 * D), F32), unroll=many)
        out_ref[...] = quarters(acc)


def side_kernel(D, H, many, place_ref, x_hbm, l_ref, r_ref, s_hbm, x_ref, s_ref, sems):
    @pl.when(place_ref[2] == 1)
    def _():
        copy = fetch(x_hbm, x_ref, sems, CHUNKS)
        for i in range(CHUNKS):
            copy(i).start()
        start = place_ref[0] * H
        per = D // CHUNKS

        @pl.when(place_ref[1] == 0)
        def _():
            rr = stacked(r_ref[...])

            def chunk(i, carry):
                copy(i).wait()
                def one(j, carry):
                    p = i * per + j
                    x = x_ref[pl.ds(aligned(2 * p + place_ref[0], H), H), :]
                    s_ref[pl.ds(p, H, stride=D), :] = product(wide(x), rr)
                    return carry

                lax.fori_loop(0, per, one, 0, unroll=min(many, per))
                return carry

            lax.fori_loop(0, CHUNKS, chunk, 0)

        @pl.when(place_ref[1] == 1)
        def _():
            ll = wide(l_ref[...].T)
            half = jnp.where(place_ref[0] == 0, ll[:H], ll[H:])

            def chunk(i, carry):
                copy(i).wait()
                def one(j, carry):
                    p = i * per + j
                    x = x_ref[pl.ds(aligned(p, D), D), :]
                    s_ref[pl.ds(p, H, stride=D), :] = product(half, stacked(x))
                    return carry

                lax.fori_loop(0, per, one, 0, unroll=min(many, per))
                return carry

            lax.fori_loop(0, CHUNKS, chunk, 0)

        done = pltpu.make_async_copy(s_ref, s_hbm, sems.at[0])
        done.start()
        done.wait()


def down_kernel(D, H, many, place_ref, x_hbm, s_hbm, e_ref, out_ref, x_ref, s_ref, n_scr, sems):
    out_ref[...] = jnp.zeros_like(out_ref)

    @pl.when(place_ref[2] == 1)
    def _():
        s_copy = fetch(s_hbm, s_ref, sems, CHUNKS)
        x_copy = fetch(x_hbm, x_ref, sems.at[pl.ds(CHUNKS, CHUNKS)], CHUNKS)
        for i in range(CHUNKS):
            s_copy(i).start()
        for i in range(CHUNKS):
            x_copy(i).start()
        start = place_ref[0] * H
        ee = wide(e_ref[...].T)
        per = 2 * H // CHUNKS

        def chunk(i, carry):
            s_copy(2 * i).wait()
            s_copy(2 * i + 1).wait()
            def one(j, carry):
                v = i * per + j
                t = s_ref[pl.ds(aligned(v, D), D), :]
                n_scr[pl.ds(v, D, stride=H), :] = product(ee, stacked(t))
                return carry

            lax.fori_loop(0, per, one, 0, unroll=min(many, per))
            return carry

        lax.fori_loop(0, CHUNKS // 2, chunk, 0)
        for i in range(CHUNKS):
            x_copy(i).wait()

        @pl.when(place_ref[1] == 0)
        def _():
            def gram(i, acc):
                q = 2 * i
                lhs = pair_rows(n_scr[pl.ds(aligned(q, H), H), :], n_scr[pl.ds(aligned(q + 1, H), H), :])
                rhs = pair_rows(x_ref[pl.ds(aligned(q, D), D), :], x_ref[pl.ds(aligned(q + 1, D), D), :])
                return acc + mm_t(lhs, rhs)

            acc = lax.fori_loop(0, D // 2, gram, jnp.zeros((2 * H, 2 * D), F32), unroll=many)
            out_ref[pl.ds(aligned(place_ref[0], H), H), :] = quarters(acc)

        @pl.when(place_ref[1] == 1)
        def _():
            def gram(i, acc):
                q = 4 * i
                v = n_scr[pl.ds(aligned(i, 4 * H), 4 * H), :].T
                lhs = jnp.concatenate(split(v), 0)
                x = [x_ref[pl.ds(pl.multiple_of((q + j) * D + start, H), H), :] for j in range(4)]
                return acc + mm(lhs, wide(jnp.concatenate(x, 0)))

            acc = lax.fori_loop(0, D // 4, gram, jnp.zeros((2 * D, 2 * D), F32), unroll=many // 2)
            out_ref[...] = quarters(acc)


def leaf_side_kernel(D, W, K, at_ref, x_hbm, xa_ref, l_ref, r_ref, t_ref, u_ref, x_ref, b_scr, sems):
    copy = fetch(x_hbm, x_ref, sems, CHUNKS)
    for i in range(CHUNKS):
        copy(i).start()
    def right(k, carry):
        rr = stacked(r_ref[k])
        for a in range(W):
            x = xa_ref[pl.ds(a, D, stride=W), :]
            t_ref[pl.ds(aligned(k * W + a, D), D), :] = product(wide(x), rr)
        return carry

    lax.fori_loop(0, K, right, 0)
    lane = lax.broadcasted_iota(jnp.int32, (W, D), 1)
    line = lax.broadcasted_iota(jnp.int32, (W, D), 0)
    pick = jnp.where(lane == line + at_ref[0] * W, 1.0, 0.0).astype(BF)
    per = D // CHUNKS

    def chunk(i, carry):
        copy(i).wait()

        def one(j, carry):
            p = i * per + j
            x = x_ref[pl.ds(aligned(p, D), D), :]
            b_scr[pl.ds(p, W, stride=D), :] = fold(mm_t(pick, jnp.concatenate(split(x), 0)))
            return carry

        return lax.fori_loop(0, per, one, carry, unroll=8)

    lax.fori_loop(0, CHUNKS, chunk, 0)

    def left(k, carry):
        ll = stacked(l_ref[k])
        for b in range(W):
            u_ref[pl.ds(aligned(k * W + b, D), D), :] = product(wide(b_scr[pl.ds(b * D, D), :]), ll)
        return carry

    lax.fori_loop(0, K, left, 0)


def leaf_kernel(D, W, K, x_hbm, t_ref, u_ref, e_ref, out_ref, x_ref, n_scr, v_scr, sems):
    copy = fetch(x_hbm, x_ref, sems, CHUNKS)
    for i in range(CHUNKS):
        copy(i).start()
    R = K * W

    def mix(k, carry):
        ee = wide(e_ref[k].T)
        for w in range(W):
            r = k * W + w
            at = pl.ds(aligned(r, D), D)
            n_scr[pl.ds(r, D, stride=R), :] = product(ee, stacked(t_ref[at, :]))
            v_scr[pl.ds(r, D, stride=R), :] = product(ee, stacked(u_ref[at, :]))
        return carry

    lax.fori_loop(0, K, mix, 0)
    def gram(i, accs):
        q = 2 * i
        one, two = pl.ds(aligned(q, R), R), pl.ds(aligned(q + 1, R), R)
        h1, l1 = split(x_ref[pl.ds(aligned(q, D), D), :])
        h2, l2 = split(x_ref[pl.ds(aligned(q + 1, D), D), :])
        cat = jnp.concatenate
        by_last = cat([cat([h1, h2], 1), cat([l1, l2], 1)], 0)
        by_first = cat([cat([h1, l1], 1), cat([h2, l2], 1)], 0)
        first = mm_t(pair_rows(n_scr[one, :], n_scr[two, :]), by_last)
        second = mm(pair_rows(v_scr[one, :], v_scr[two, :]), by_first)
        return accs[0] + first, accs[1] + second

    zero = jnp.zeros((2 * R, 2 * D), F32)
    count = D // (2 * CHUNKS)

    def chunk(i, accs):
        copy(i).wait()
        return lax.fori_loop(0, count, lambda j, a: gram(i * count + j, a), accs, unroll=4)

    first, second = lax.fori_loop(0, CHUNKS, chunk, (zero, zero))
    first = quarters(first)
    second = quarters(second)
    for k in range(K):
        out_ref[k, 0] = first[k * W : (k + 1) * W]
        out_ref[k, 1] = second[k * W : (k + 1) * W]


VMEM = pl.BlockSpec(memory_space=pltpu.VMEM)
SMEM = pl.BlockSpec(memory_space=pltpu.SMEM)
HBM = pl.BlockSpec(memory_space=pltpu.HBM)


def call(kernel, name, mib, units, out_shape, in_specs, out_specs, scratch):
    return pl.pallas_call(
        kernel,
        out_shape=out_shape,
        in_specs=in_specs,
        out_specs=out_specs,
        scratch_shapes=scratch,
        compiler_params=pltpu.CompilerParams(vmem_limit_bytes=mib << 20),
        cost_estimate=pl.CostEstimate(
            flops=int(units * 4.8e9), bytes_accessed=8 << 20, transcendentals=0
        ),
        name=name,
    )


def up_rows(place, tensor, left_env, right_env, many=16):
    D = left_env.shape[0]
    H = D // 2
    return call(
        functools.partial(up_kernel, D, H, many),
        "up",
        57,
        1,
        jax.ShapeDtypeStruct((H, D), F32),
        [SMEM, HBM, VMEM, VMEM],
        VMEM,
        [pltpu.VMEM((D * D, D), F32), pltpu.VMEM((D * H, D), F32), pltpu.SemaphoreType.DMA((2 * CHUNKS,))],
    )(place, tensor.reshape(D * D, D), left_env, right_env)


def side_part(place, tensor, left_env, right_env, many=8):
    D = left_env.shape[0]
    H = D // 2
    return call(
        functools.partial(side_kernel, D, H, many),
        "side",
        57,
        0.4,
        jax.ShapeDtypeStruct((D * H, D), F32),
        [SMEM, HBM, VMEM, VMEM],
        HBM,
        [pltpu.VMEM((D * D, D), F32), pltpu.VMEM((D * H, D), F32), pltpu.SemaphoreType.DMA((CHUNKS,))],
    )(place, tensor.reshape(D * D, D), left_env, right_env)


def down_part(place, tensor, side, above, many=16):
    D = above.shape[0]
    H = D // 2
    big = pltpu.VMEM((D * D, D), F32)
    half = pltpu.VMEM((D * H, D), F32)
    return call(
        functools.partial(down_kernel, D, H, many),
        "down",
        57,
        0.7,
        jax.ShapeDtypeStruct((D, D), F32),
        [SMEM, HBM, HBM, VMEM],
        VMEM,
        [big, half, half, pltpu.SemaphoreType.DMA((2 * CHUNKS,))],
    )(place, tensor.reshape(D * D, D), side, above)


def leaf_sides(at, whole, slab, left, right):
    K, D = left.shape[:2]
    W = slab.shape[1]
    rows = jax.ShapeDtypeStruct((K * W * D, D), F32)
    return call(
        functools.partial(leaf_side_kernel, D, W, K),
        "leaf_side",
        57,
        0.7,
        (rows, rows),
        [SMEM, HBM, VMEM, VMEM, VMEM],
        (VMEM, VMEM),
        [pltpu.VMEM((D * D, D), F32), pltpu.VMEM((W * D, D), F32), pltpu.SemaphoreType.DMA((CHUNKS,))],
    )(at.reshape(1), whole.reshape(D * D, D), slab.reshape(D * W, D), left, right)


def leaf_rows(whole, sides, above):
    K, D = above.shape[:2]
    W = sides[0].shape[0] // (K * D)
    rows = pltpu.VMEM((K * W * D, D), F32)
    return call(
        functools.partial(leaf_kernel, D, W, K),
        "leaf",
        57,
        0.7,
        jax.ShapeDtypeStruct((K, 2, W, D), F32),
        [HBM, VMEM, VMEM, VMEM],
        VMEM,
        [pltpu.VMEM((D * D, D), F32), rows, rows, pltpu.SemaphoreType.DMA((CHUNKS,))],
    )(whole.reshape(D * D, D), sides[0], sides[1], above)


NODE = ("ylo", "zhi", "zlo")
BOND = ("yhi", "x", "core")
SLOT_OF = (4, 2, 5, 1, 6, 3, 7, 0)


def ein(spec, a, b):
    return jnp.einsum(spec, a, b, precision=lax.Precision.HIGHEST)


def after(x, other):
    return lax.optimization_barrier((x, other))[0]


def other_core(x):
    return lax.ppermute(x, "core", [(0, 1), (1, 0)])


def join_cores(half, core, axis):
    other = other_core(half)
    low = jnp.where(core == 0, half, other)
    high = jnp.where(core == 0, other, half)
    return jnp.concatenate([low, high], axis=axis)


def reorder_kernel(in_ref, out_ref):
    for g, s in enumerate(SLOT_OF):
        out_ref[g] = in_ref[s]


def reordered(x):
    return pl.pallas_call(
        reorder_kernel,
        out_shape=jax.ShapeDtypeStruct(x.shape, x.dtype),
        in_specs=[VMEM],
        out_specs=VMEM,
        compiler_params=pltpu.CompilerParams(vmem_limit_bytes=8 << 20),
        name="reorder",
    )(x)


def local(bottom_nodes, upper_nodes, leaf_up, outside_env, top_env):
    group = lax.axis_index(NODE)
    bond = lax.axis_index(BOND)
    core = lax.axis_index("core")
    yhi = lax.axis_index("yhi")
    op = jnp.minimum(lax.axis_index("x"), 2)
    width = bottom_nodes.shape[2]
    rows = bottom_nodes.shape[1]
    parts = width // rows

    got = lax.all_to_all(reordered(upper_nodes), NODE, 0, 0, tiled=True)
    shard = jnp.moveaxis(got, 0, 1).reshape(rows, width, width)
    upper = lax.all_gather(shard, BOND, axis=0, tiled=True)

    mine = bottom_nodes[0]
    left_leaf = leaf_up[0, :, 0]
    right_leaf = leaf_up[0, :, 1]
    middle = ein("kac,pcd->kpad", left_leaf, after(mine, shard))
    product = ein("kpad,kbd->kpab", middle, right_leaf)
    both = jnp.concatenate([mine[None], product])
    both = jnp.moveaxis(both.reshape(4, rows, parts, rows, width), 2, 0)
    both = lax.all_to_all(both, BOND, 0, 0, tiled=True)
    both = jnp.moveaxis(both, 1, 0).reshape(4, width, rows, width)
    mine_a = both[0]
    gram = ein("pab,kqab->kpq", mine_a, both[1:])
    pieces = jnp.moveaxis(gram.reshape(3, parts, rows, width), 1, 0)
    pieces = lax.all_to_all(pieces, BOND, 0, 0, tiled=True)
    env = jnp.sum(pieces, axis=0)
    by_x = jnp.stack([env[0], env[1], env[2], env[2]])
    by_dest = jnp.broadcast_to(by_x[None, None, :, None], (2, 2, 4, 2, rows, width))
    by_dest = by_dest.reshape(2 * parts, rows, width)
    pair = lax.all_to_all(by_dest, ("zlo",) + BOND, 0, 0, tiled=True)
    left3, right3 = pair.reshape(2, width, width)

    def move(x, *pairs):
        return lax.ppermute(x, NODE, pairs)

    def place(active, which=jnp.int32(0)):
        return jnp.stack([core, which, active.astype(jnp.int32)])

    is_third = group % 2 == 0
    is_second = (group == 1) | (group == 5)
    is_first = group == 3

    whole = lax.all_gather(after(mine, left3), BOND, axis=0, tiled=True)
    sides = leaf_sides(bond, whole, mine_a, left_leaf, right_leaf)

    up2 = up_rows(place(is_third), upper, left3, right3)
    ends = jnp.stack([move(up2, (0, 1), (4, 5)), move(up2, (2, 1), (6, 5))])
    left2, right2 = join_cores(ends, core, 1)
    top = lax.dynamic_index_in_dim(top_env, op, 0, keepdims=False)
    outside = lax.dynamic_index_in_dim(outside_env, op, 0, keepdims=False)
    at_crown = place(group == 7)
    crown = side_part(at_crown, upper, outside, outside, 4)
    crown = down_part(at_crown, upper, crown, top, 4)
    crown = move(crown, (7, 3))
    crown = crown + other_core(crown)
    side3 = side_part(place(is_third, yhi), upper, left3, right3, 4)
    left2, right2, side3 = lax.optimization_barrier((left2, right2, side3))
    up1 = up_rows(place(is_second), upper, left2, right2)
    ends = jnp.stack([move(up1, (1, 3)), move(up1, (5, 3))])
    left1, right1 = join_cores(ends, core, 1)
    side2 = side_part(place(is_second, yhi), upper, left2, right2, 4)
    left1, right1, side2 = lax.optimization_barrier((left1, right1, side2))

    def send_both(x, straight, across):
        axes = NODE + ("yhi",)
        return lax.ppermute(x, axes, straight), lax.ppermute(x, axes, across)

    def family(parent, one, two):
        straight = [(2 * parent, 2 * one), (2 * parent + 1, 2 * two + 1)]
        across = [(2 * parent, 2 * one + 1), (2 * parent + 1, 2 * two)]
        return straight, across

    at_first = place(is_first, yhi)
    side1 = side_part(at_first, upper, left1, right1, 16)
    made = down_part(at_first, upper, side1, crown)
    one, two = send_both(made, *family(3, 1, 5))
    above = one + two
    above = above + other_core(above)
    root = up_rows(place(is_first), upper, left1, after(right1, made), 4)
    root = join_cores(root, core, 0)
    made = down_part(place(is_second, yhi), upper, side2, above)

    fa, fb = family(1, 0, 2), family(5, 4, 6)
    one, two = send_both(
        jnp.where(is_first, root, made),
        fa[0] + fb[0] + [(6, 14), (7, 15)],
        fa[1] + fb[1] + [(6, 2), (7, 3)],
    )
    one, two, *sides = lax.optimization_barrier((one, two, *sides))
    root = jnp.where(group == 7, one, jnp.where(group == 1, two, root))
    above = one + two
    above = above + other_core(above)
    made = down_part(place(is_third, yhi), upper, side3, above)
    straight = [(1, 3), (5, 7), (9, 11), (13, 15), (0, 1), (4, 5), (8, 9), (12, 13)]
    across = [(1, 2), (5, 6), (9, 10), (13, 14)]
    straight += [(2, 0), (3, 4), (6, 8), (14, 12), (15, 10)]
    across += [(2, 1), (3, 5), (6, 9), (14, 13), (15, 11)]
    one, two = send_both(jnp.where(is_third, made, root), straight, across)
    has_root = (group == 1) | (group == 3) | (group == 7)
    root = jnp.where(has_root, root, jnp.where(yhi == 0, one, two))
    kept = jnp.where(is_third, made, two)
    last = jnp.where(yhi == 0, kept, one)
    last = last + other_core(last)
    ends = lax.all_gather(jnp.stack([last, root]), "x", axis=0, tiled=False)
    above = ends[:3, 0]
    root_env = ends[:3, 1]
    return leaf_rows(whole, sides, above)[None], root_env


def solution(mesh):
    shape = (2, 2, 2, 2, 4, 2)
    fine = Mesh(mesh.devices.reshape(shape), NODE + BOND)
    placed = (
        P(NODE, BOND, None, None),
        P(None, BOND, NODE, None),
        P(NODE, None, None, None, None),
        P(),
        P(),
    )
    return jax.shard_map(
        local,
        mesh=fine,
        in_specs=placed,
        out_specs=(P(NODE, None, None, BOND, None), P()),
        check_vma=False,
    )
```

```python
import functools

import jax
import jax.numpy as jnp
from jax import lax
from jax.experimental import pallas as pl
from jax.experimental.pallas import tpu as pltpu
from jax.sharding import Mesh, PartitionSpec as P

BF = jnp.bfloat16
F32 = jnp.float32
CHUNKS = 8


def split(v):
    hi = v.astype(BF)
    return hi, (v - hi.astype(F32)).astype(BF)


def wide(v):
    return jnp.concatenate(split(v), axis=1)


def stacked(v):
    row = wide(v)
    return jnp.concatenate([row, row], axis=0)


def mm(a, b):
    return jnp.dot(a, b, preferred_element_type=F32)


def mm_t(a, b):
    return lax.dot_general(a, b, (((1,), (1,)), ((), ())), preferred_element_type=F32)


def fold(v):
    half = v.shape[1] // 2
    return v[:, :half] + v[:, half:]


def product(a_wide, b_stacked):
    return fold(mm(a_wide, b_stacked))


def pair_rows(one, two):
    h1, l1 = split(one)
    h2, l2 = split(two)
    return jnp.concatenate([jnp.concatenate([h1, h2], 1), jnp.concatenate([l1, l2], 1)], 0)


def quarters(acc):
    r = acc.shape[0] // 2
    c = acc.shape[1] // 2
    return (acc[:r, :c] + acc[r:, :c]) + (acc[:r, c:] + acc[r:, c:])


def aligned(i, n):
    return pl.multiple_of(i * n, n)


def fetch(src, dst, sems, count, first=0):
    size = dst.shape[0] // count

    def copy(i):
        at = lax.rem(first + i, count)
        there = pl.ds(aligned(at, size), size)
        return pltpu.make_async_copy(src.at[there], dst.at[there], sems.at[i])

    return copy


def up_kernel(D, H, many, place_ref, x_hbm, l_ref, r_ref, out_ref, x_ref, n_scr, sems):
    @pl.when(place_ref[2] == 0)
    def _():
        out_ref[...] = jnp.zeros_like(out_ref)

    @pl.when(place_ref[2] == 1)
    def _():
        count = 2 * CHUNKS
        copy = fetch(x_hbm, x_ref, sems, count, place_ref[0] * CHUNKS)
        for i in range(count):
            copy(i).start()
        start = place_ref[0] * H
        rr = stacked(r_ref[...])
        ll = wide(l_ref[...].T)
        per = 2 * H // CHUNKS

        def chunk(i, carry):
            copy(2 * i).wait()
            copy(2 * i + 1).wait()
            def one(j, carry):
                p = i * per + j
                t = product(wide(x_ref[pl.ds(aligned(start + p, D), D), :]), rr)
                n_scr[pl.ds(p, D, stride=H), :] = product(ll, stacked(t))
                return carry

            lax.fori_loop(0, per, one, 0, unroll=min(many, per))
            return carry

        lax.fori_loop(0, CHUNKS // 2, chunk, 0)
        for i in range(CHUNKS, count):
            copy(i).wait()

        def gram(i, acc):
            c = 2 * i
            lhs = pair_rows(n_scr[pl.ds(aligned(c, H), H), :], n_scr[pl.ds(aligned(c + 1, H), H), :])
            rhs = pair_rows(x_ref[pl.ds(c, D, stride=D), :], x_ref[pl.ds(c + 1, D, stride=D), :])
            return acc + mm_t(lhs, rhs)

        acc = lax.fori_loop(0, D // 2, gram, jnp.zeros((2 * H, 2 * D), F32), unroll=many)
        out_ref[...] = quarters(acc)


def side_kernel(D, H, many, place_ref, x_hbm, l_ref, r_ref, s_hbm, x_ref, s_ref, sems):
    @pl.when(place_ref[2] == 1)
    def _():
        copy = fetch(x_hbm, x_ref, sems, CHUNKS)
        for i in range(CHUNKS):
            copy(i).start()
        start = place_ref[0] * H
        per = D // CHUNKS

        @pl.when(place_ref[1] == 0)
        def _():
            rr = stacked(r_ref[...])

            def chunk(i, carry):
                copy(i).wait()
                def one(j, carry):
                    p = i * per + j
                    x = x_ref[pl.ds(aligned(2 * p + place_ref[0], H), H), :]
                    s_ref[pl.ds(p, H, stride=D), :] = product(wide(x), rr)
                    return carry

                lax.fori_loop(0, per, one, 0, unroll=min(many, per))
                return carry

            lax.fori_loop(0, CHUNKS, chunk, 0)

        @pl.when(place_ref[1] == 1)
        def _():
            ll = wide(l_ref[...].T)
            half = jnp.where(place_ref[0] == 0, ll[:H], ll[H:])

            def chunk(i, carry):
                copy(i).wait()
                def one(j, carry):
                    p = i * per + j
                    x = x_ref[pl.ds(aligned(p, D), D), :]
                    s_ref[pl.ds(p, H, stride=D), :] = product(half, stacked(x))
                    return carry

                lax.fori_loop(0, per, one, 0, unroll=min(many, per))
                return carry

            lax.fori_loop(0, CHUNKS, chunk, 0)

        done = pltpu.make_async_copy(s_ref, s_hbm, sems.at[0])
        done.start()
        done.wait()


def down_kernel(D, H, many, place_ref, x_hbm, s_hbm, e_ref, out_ref, x_ref, s_ref, n_scr, sems):
    out_ref[...] = jnp.zeros_like(out_ref)

    @pl.when(place_ref[2] == 1)
    def _():
        s_copy = fetch(s_hbm, s_ref, sems, CHUNKS)
        x_copy = fetch(x_hbm, x_ref, sems.at[pl.ds(CHUNKS, CHUNKS)], CHUNKS)
        for i in range(CHUNKS):
            s_copy(i).start()
        for i in range(CHUNKS):
            x_copy(i).start()
        start = place_ref[0] * H
        ee = wide(e_ref[...].T)
        per = 2 * H // CHUNKS

        def chunk(i, carry):
            s_copy(2 * i).wait()
            s_copy(2 * i + 1).wait()
            def one(j, carry):
                v = i * per + j
                t = s_ref[pl.ds(aligned(v, D), D), :]
                n_scr[pl.ds(v, D, stride=H), :] = product(ee, stacked(t))
                return carry

            lax.fori_loop(0, per, one, 0, unroll=min(many, per))
            return carry

        lax.fori_loop(0, CHUNKS // 2, chunk, 0)
        for i in range(CHUNKS):
            x_copy(i).wait()

        @pl.when(place_ref[1] == 0)
        def _():
            def gram(i, acc):
                q = 2 * i
                lhs = pair_rows(n_scr[pl.ds(aligned(q, H), H), :], n_scr[pl.ds(aligned(q + 1, H), H), :])
                rhs = pair_rows(x_ref[pl.ds(aligned(q, D), D), :], x_ref[pl.ds(aligned(q + 1, D), D), :])
                return acc + mm_t(lhs, rhs)

            acc = lax.fori_loop(0, D // 2, gram, jnp.zeros((2 * H, 2 * D), F32), unroll=2 * many)
            out_ref[pl.ds(aligned(place_ref[0], H), H), :] = quarters(acc)

        @pl.when(place_ref[1] == 1)
        def _():
            def gram(i, acc):
                q = 4 * i
                v = n_scr[pl.ds(aligned(i, 4 * H), 4 * H), :].T
                lhs = jnp.concatenate(split(v), 0)
                x = [x_ref[pl.ds(pl.multiple_of((q + j) * D + start, H), H), :] for j in range(4)]
                return acc + mm(lhs, wide(jnp.concatenate(x, 0)))

            acc = lax.fori_loop(0, D // 4, gram, jnp.zeros((2 * D, 2 * D), F32), unroll=many)
            out_ref[...] = quarters(acc)


def leaf_side_kernel(D, W, K, at_ref, x_hbm, xa_ref, l_ref, r_ref, t_ref, u_ref, x_ref, b_scr, sems):
    copy = fetch(x_hbm, x_ref, sems, CHUNKS)
    for i in range(CHUNKS):
        copy(i).start()
    def right(k, carry):
        rr = stacked(r_ref[k])
        for a in range(W):
            x = xa_ref[pl.ds(a, D, stride=W), :]
            t_ref[pl.ds(aligned(k * W + a, D), D), :] = product(wide(x), rr)
        return carry

    lax.fori_loop(0, K, right, 0)
    lane = lax.broadcasted_iota(jnp.int32, (W, D), 1)
    line = lax.broadcasted_iota(jnp.int32, (W, D), 0)
    pick = jnp.where(lane == line + at_ref[0] * W, 1.0, 0.0).astype(BF)
    per = D // CHUNKS

    def chunk(i, carry):
        copy(i).wait()

        def one(j, carry):
            p = i * per + j
            x = x_ref[pl.ds(aligned(p, D), D), :]
            b_scr[pl.ds(p, W, stride=D), :] = fold(mm_t(pick, jnp.concatenate(split(x), 0)))
            return carry

        return lax.fori_loop(0, per, one, carry, unroll=8)

    lax.fori_loop(0, CHUNKS, chunk, 0)

    def left(k, carry):
        ll = stacked(l_ref[k])
        for b in range(W):
            u_ref[pl.ds(aligned(k * W + b, D), D), :] = product(wide(b_scr[pl.ds(b * D, D), :]), ll)
        return carry

    lax.fori_loop(0, K, left, 0)


def leaf_kernel(D, W, K, x_hbm, t_ref, u_ref, e_ref, out_ref, x_ref, n_scr, v_scr, sems):
    copy = fetch(x_hbm, x_ref, sems, CHUNKS)
    for i in range(CHUNKS):
        copy(i).start()
    R = K * W

    def mix(k, carry):
        ee = wide(e_ref[k].T)
        for w in range(W):
            r = k * W + w
            at = pl.ds(aligned(r, D), D)
            n_scr[pl.ds(r, D, stride=R), :] = product(ee, stacked(t_ref[at, :]))
            v_scr[pl.ds(r, D, stride=R), :] = product(ee, stacked(u_ref[at, :]))
        return carry

    lax.fori_loop(0, K, mix, 0)
    def gram(i, accs):
        q = 2 * i
        one, two = pl.ds(aligned(q, R), R), pl.ds(aligned(q + 1, R), R)
        h1, l1 = split(x_ref[pl.ds(aligned(q, D), D), :])
        h2, l2 = split(x_ref[pl.ds(aligned(q + 1, D), D), :])
        cat = jnp.concatenate
        by_last = cat([cat([h1, h2], 1), cat([l1, l2], 1)], 0)
        by_first = cat([cat([h1, l1], 1), cat([h2, l2], 1)], 0)
        first = mm_t(pair_rows(n_scr[one, :], n_scr[two, :]), by_last)
        second = mm(pair_rows(v_scr[one, :], v_scr[two, :]), by_first)
        return accs[0] + first, accs[1] + second

    zero = jnp.zeros((2 * R, 2 * D), F32)
    count = D // (2 * CHUNKS)

    def chunk(i, accs):
        copy(i).wait()
        return lax.fori_loop(0, count, lambda j, a: gram(i * count + j, a), accs, unroll=4)

    first, second = lax.fori_loop(0, CHUNKS, chunk, (zero, zero))
    first = quarters(first)
    second = quarters(second)
    for k in range(K):
        out_ref[k, 0] = first[k * W : (k + 1) * W]
        out_ref[k, 1] = second[k * W : (k + 1) * W]


VMEM = pl.BlockSpec(memory_space=pltpu.VMEM)
SMEM = pl.BlockSpec(memory_space=pltpu.SMEM)
HBM = pl.BlockSpec(memory_space=pltpu.HBM)


def call(kernel, name, mib, units, out_shape, in_specs, out_specs, scratch):
    return pl.pallas_call(
        kernel,
        out_shape=out_shape,
        in_specs=in_specs,
        out_specs=out_specs,
        scratch_shapes=scratch,
        compiler_params=pltpu.CompilerParams(vmem_limit_bytes=mib << 20),
        cost_estimate=pl.CostEstimate(
            flops=int(units * 4.8e9), bytes_accessed=8 << 20, transcendentals=0
        ),
        name=name,
    )


def up_rows(place, tensor, left_env, right_env, many=16):
    D = left_env.shape[0]
    H = D // 2
    return call(
        functools.partial(up_kernel, D, H, many),
        "up",
        57,
        1,
        jax.ShapeDtypeStruct((H, D), F32),
        [SMEM, HBM, VMEM, VMEM],
        VMEM,
        [pltpu.VMEM((D * D, D), F32), pltpu.VMEM((D * H, D), F32), pltpu.SemaphoreType.DMA((2 * CHUNKS,))],
    )(place, tensor.reshape(D * D, D), left_env, right_env)


def side_part(place, tensor, left_env, right_env, many=8):
    D = left_env.shape[0]
    H = D // 2
    return call(
        functools.partial(side_kernel, D, H, many),
        "side",
        57,
        0.4,
        jax.ShapeDtypeStruct((D * H, D), F32),
        [SMEM, HBM, VMEM, VMEM],
        HBM,
        [pltpu.VMEM((D * D, D), F32), pltpu.VMEM((D * H, D), F32), pltpu.SemaphoreType.DMA((CHUNKS,))],
    )(place, tensor.reshape(D * D, D), left_env, right_env)


def down_part(place, tensor, side, above, many=16):
    D = above.shape[0]
    H = D // 2
    big = pltpu.VMEM((D * D, D), F32)
    half = pltpu.VMEM((D * H, D), F32)
    return call(
        functools.partial(down_kernel, D, H, many),
        "down",
        57,
        0.7,
        jax.ShapeDtypeStruct((D, D), F32),
        [SMEM, HBM, HBM, VMEM],
        VMEM,
        [big, half, half, pltpu.SemaphoreType.DMA((2 * CHUNKS,))],
    )(place, tensor.reshape(D * D, D), side, above)


def leaf_sides(at, whole, slab, left, right):
    K, D = left.shape[:2]
    W = slab.shape[1]
    rows = jax.ShapeDtypeStruct((K * W * D, D), F32)
    return call(
        functools.partial(leaf_side_kernel, D, W, K),
        "leaf_side",
        57,
        0.7,
        (rows, rows),
        [SMEM, HBM, VMEM, VMEM, VMEM],
        (VMEM, VMEM),
        [pltpu.VMEM((D * D, D), F32), pltpu.VMEM((W * D, D), F32), pltpu.SemaphoreType.DMA((CHUNKS,))],
    )(at.reshape(1), whole.reshape(D * D, D), slab.reshape(D * W, D), left, right)


def leaf_rows(whole, sides, above):
    K, D = above.shape[:2]
    W = sides[0].shape[0] // (K * D)
    rows = pltpu.VMEM((K * W * D, D), F32)
    return call(
        functools.partial(leaf_kernel, D, W, K),
        "leaf",
        57,
        0.7,
        jax.ShapeDtypeStruct((K, 2, W, D), F32),
        [HBM, VMEM, VMEM, VMEM],
        VMEM,
        [pltpu.VMEM((D * D, D), F32), rows, rows, pltpu.SemaphoreType.DMA((CHUNKS,))],
    )(whole.reshape(D * D, D), sides[0], sides[1], above)


NODE = ("ylo", "zhi", "zlo")
BOND = ("yhi", "x", "core")
SLOT_OF = (4, 2, 5, 1, 6, 3, 7, 0)


def ein(spec, a, b):
    return jnp.einsum(spec, a, b, precision=lax.Precision.HIGHEST)


def after(x, other):
    return lax.optimization_barrier((x, other))[0]


def other_core(x):
    return lax.ppermute(x, "core", [(0, 1), (1, 0)])


def join_cores(half, core, axis):
    other = other_core(half)
    low = jnp.where(core == 0, half, other)
    high = jnp.where(core == 0, other, half)
    return jnp.concatenate([low, high], axis=axis)


def reorder_kernel(in_ref, out_ref):
    for g, s in enumerate(SLOT_OF):
        out_ref[g] = in_ref[s]


def reordered(x):
    return pl.pallas_call(
        reorder_kernel,
        out_shape=jax.ShapeDtypeStruct(x.shape, x.dtype),
        in_specs=[VMEM],
        out_specs=VMEM,
        compiler_params=pltpu.CompilerParams(vmem_limit_bytes=8 << 20),
        name="reorder",
    )(x)


def local(bottom_nodes, upper_nodes, leaf_up, outside_env, top_env):
    group = lax.axis_index(NODE)
    bond = lax.axis_index(BOND)
    core = lax.axis_index("core")
    yhi = lax.axis_index("yhi")
    op = jnp.minimum(lax.axis_index("x"), 2)
    width = bottom_nodes.shape[2]
    rows = bottom_nodes.shape[1]
    parts = width // rows

    got = lax.all_to_all(reordered(upper_nodes), NODE, 0, 0, tiled=True)
    shard = jnp.moveaxis(got, 0, 1).reshape(rows, width, width)
    upper = lax.all_gather(shard, BOND, axis=0, tiled=True)

    mine = bottom_nodes[0]
    left_leaf = leaf_up[0, :, 0]
    right_leaf = leaf_up[0, :, 1]
    middle = ein("kac,pcd->kpad", left_leaf, after(mine, shard))
    product = ein("kpad,kbd->kpab", middle, right_leaf)
    both = jnp.concatenate([mine[None], product])
    both = jnp.moveaxis(both.reshape(4, rows, parts, rows, width), 2, 0)
    both = lax.all_to_all(both, BOND, 0, 0, tiled=True)
    both = jnp.moveaxis(both, 1, 0).reshape(4, width, rows, width)
    mine_a = both[0]
    gram = ein("pab,kqab->kpq", mine_a, both[1:])
    pieces = jnp.moveaxis(gram.reshape(3, parts, rows, width), 1, 0)
    pieces = lax.all_to_all(pieces, BOND, 0, 0, tiled=True)
    env = jnp.sum(pieces, axis=0)
    by_x = jnp.stack([env[0], env[1], env[2], env[2]])
    by_dest = jnp.broadcast_to(by_x[None, None, :, None], (2, 2, 4, 2, rows, width))
    by_dest = by_dest.reshape(2 * parts, rows, width)
    pair = lax.all_to_all(by_dest, ("zlo",) + BOND, 0, 0, tiled=True)
    left3, right3 = pair.reshape(2, width, width)

    def move(x, *pairs):
        return lax.ppermute(x, NODE, pairs)

    def place(active, which=jnp.int32(0)):
        return jnp.stack([core, which, active.astype(jnp.int32)])

    is_third = group % 2 == 0
    is_second = (group == 1) | (group == 5)
    is_first = group == 3

    whole = lax.all_gather(after(mine, left3), BOND, axis=0, tiled=True)
    sides = leaf_sides(bond, whole, mine_a, left_leaf, right_leaf)

    up2 = up_rows(place(is_third), upper, left3, right3)
    ends = jnp.stack([move(up2, (0, 1), (4, 5)), move(up2, (2, 1), (6, 5))])
    left2, right2 = join_cores(ends, core, 1)
    top = lax.dynamic_index_in_dim(top_env, op, 0, keepdims=False)
    outside = lax.dynamic_index_in_dim(outside_env, op, 0, keepdims=False)
    at_crown = place(group == 7)
    crown = side_part(at_crown, upper, outside, outside, 4)
    crown = down_part(at_crown, upper, crown, top, 4)
    crown = move(crown, (7, 3))
    crown = crown + other_core(crown)
    side3 = side_part(place(is_third, yhi), upper, left3, right3, 4)
    left2, right2, side3 = lax.optimization_barrier((left2, right2, side3))
    up1 = up_rows(place(is_second), upper, left2, right2)
    ends = jnp.stack([move(up1, (1, 3)), move(up1, (5, 3))])
    left1, right1 = join_cores(ends, core, 1)
    side2 = side_part(place(is_second, yhi), upper, left2, right2, 4)
    left1, right1, side2 = lax.optimization_barrier((left1, right1, side2))

    def send_both(x, straight, across):
        axes = NODE + ("yhi",)
        return lax.ppermute(x, axes, straight), lax.ppermute(x, axes, across)

    def family(parent, one, two):
        straight = [(2 * parent, 2 * one), (2 * parent + 1, 2 * two + 1)]
        across = [(2 * parent, 2 * one + 1), (2 * parent + 1, 2 * two)]
        return straight, across

    at_first = place(is_first, yhi)
    side1 = side_part(at_first, upper, left1, right1, 16)
    made = down_part(at_first, upper, side1, crown)
    one, two = send_both(made, *family(3, 1, 5))
    above = one + two
    above = above + other_core(above)
    root = up_rows(place(is_first), upper, left1, after(right1, made), 4)
    root = join_cores(root, core, 0)
    made = down_part(place(is_second, yhi), upper, side2, above)

    fa, fb = family(1, 0, 2), family(5, 4, 6)
    one, two = send_both(
        jnp.where(is_first, root, made),
        fa[0] + fb[0] + [(6, 14), (7, 15)],
        fa[1] + fb[1] + [(6, 2), (7, 3)],
    )
    one, two, *sides = lax.optimization_barrier((one, two, *sides))
    root = jnp.where(group == 7, one, jnp.where(group == 1, two, root))
    above = one + two
    above = above + other_core(above)
    made = down_part(place(is_third, yhi), upper, side3, above)
    straight = [(1, 3), (5, 7), (9, 11), (13, 15), (0, 1), (4, 5), (8, 9), (12, 13)]
    across = [(1, 2), (5, 6), (9, 10), (13, 14)]
    straight += [(2, 0), (3, 4), (6, 8), (14, 12), (15, 10)]
    across += [(2, 1), (3, 5), (6, 9), (14, 13), (15, 11)]
    one, two = send_both(jnp.where(is_third, made, root), straight, across)
    has_root = (group == 1) | (group == 3) | (group == 7)
    root = jnp.where(has_root, root, jnp.where(yhi == 0, one, two))
    kept = jnp.where(is_third, made, two)
    last = jnp.where(yhi == 0, kept, one)
    last = last + other_core(last)
    ends = lax.all_gather(jnp.stack([last, root]), "x", axis=0, tiled=False)
    above = ends[:3, 0]
    root_env = ends[:3, 1]
    return leaf_rows(whole, sides, above)[None], root_env


def solution(mesh):
    shape = (2, 2, 2, 2, 4, 2)
    fine = Mesh(mesh.devices.reshape(shape), NODE + BOND)
    placed = (
        P(NODE, BOND, None, None),
        P(None, BOND, NODE, None),
        P(NODE, None, None, None, None),
        P(),
        P(),
    )
    return jax.shard_map(
        local,
        mesh=fine,
        in_specs=placed,
        out_specs=(P(NODE, None, None, BOND, None), P()),
        check_vma=False,
    )
```

```python
import functools

import jax
import jax.numpy as jnp
from jax import lax
from jax.experimental import pallas as pl
from jax.experimental.pallas import tpu as pltpu
from jax.sharding import Mesh, PartitionSpec as P

BF = jnp.bfloat16
F32 = jnp.float32
CHUNKS = 8


def split(v):
    hi = v.astype(BF)
    return hi, (v - hi.astype(F32)).astype(BF)


def wide(v):
    return jnp.concatenate(split(v), axis=1)


def stacked(v):
    row = wide(v)
    return jnp.concatenate([row, row], axis=0)


def mm(a, b):
    return jnp.dot(a, b, preferred_element_type=F32)


def mm_t(a, b):
    return lax.dot_general(a, b, (((1,), (1,)), ((), ())), preferred_element_type=F32)


def fold(v):
    half = v.shape[1] // 2
    return v[:, :half] + v[:, half:]


def product(a_wide, b_stacked):
    return fold(mm(a_wide, b_stacked))


def pair_rows(one, two):
    h1, l1 = split(one)
    h2, l2 = split(two)
    return jnp.concatenate([jnp.concatenate([h1, h2], 1), jnp.concatenate([l1, l2], 1)], 0)


def quarters(acc):
    r = acc.shape[0] // 2
    c = acc.shape[1] // 2
    return (acc[:r, :c] + acc[r:, :c]) + (acc[:r, c:] + acc[r:, c:])


def aligned(i, n):
    return pl.multiple_of(i * n, n)


def fetch(src, dst, sems, count, first=0):
    size = dst.shape[0] // count

    def copy(i):
        at = lax.rem(first + i, count)
        there = pl.ds(aligned(at, size), size)
        return pltpu.make_async_copy(src.at[there], dst.at[there], sems.at[i])

    return copy


def up_kernel(D, H, many, place_ref, x_hbm, l_ref, r_ref, out_ref, x_ref, n_scr, sems):
    @pl.when(place_ref[2] == 0)
    def _():
        out_ref[...] = jnp.zeros_like(out_ref)

    @pl.when(place_ref[2] == 1)
    def _():
        count = 2 * CHUNKS
        copy = fetch(x_hbm, x_ref, sems, count, place_ref[0] * CHUNKS)
        for i in range(count):
            copy(i).start()
        start = place_ref[0] * H
        rr = stacked(r_ref[...])
        ll = wide(l_ref[...].T)
        per = 2 * H // CHUNKS

        def chunk(i, carry):
            copy(2 * i).wait()
            copy(2 * i + 1).wait()
            def one(j, carry):
                p = i * per + j
                t = product(wide(x_ref[pl.ds(aligned(start + p, D), D), :]), rr)
                n_scr[pl.ds(p, D, stride=H), :] = product(ll, stacked(t))
                return carry

            lax.fori_loop(0, per, one, 0, unroll=min(many, per))
            return carry

        lax.fori_loop(0, CHUNKS // 2, chunk, 0)
        for i in range(CHUNKS, count):
            copy(i).wait()

        def gram(i, acc):
            c = 2 * i
            lhs = pair_rows(n_scr[pl.ds(aligned(c, H), H), :], n_scr[pl.ds(aligned(c + 1, H), H), :])
            rhs = pair_rows(x_ref[pl.ds(c, D, stride=D), :], x_ref[pl.ds(c + 1, D, stride=D), :])
            return acc + mm_t(lhs, rhs)

        acc = lax.fori_loop(0, D // 2, gram, jnp.zeros((2 * H, 2 * D), F32), unroll=many)
        out_ref[...] = quarters(acc)


def side_kernel(D, H, many, place_ref, x_hbm, l_ref, r_ref, s_hbm, x_ref, s_ref, sems):
    @pl.when(place_ref[2] == 1)
    def _():
        copy = fetch(x_hbm, x_ref, sems, CHUNKS)
        for i in range(CHUNKS):
            copy(i).start()
        start = place_ref[0] * H
        per = D // CHUNKS

        @pl.when(place_ref[1] == 0)
        def _():
            rr = stacked(r_ref[...])

            def chunk(i, carry):
                copy(i).wait()
                def one(j, carry):
                    p = i * per + j
                    x = x_ref[pl.ds(aligned(2 * p + place_ref[0], H), H), :]
                    s_ref[pl.ds(p, H, stride=D), :] = product(wide(x), rr)
                    return carry

                lax.fori_loop(0, per, one, 0, unroll=min(many, per))
                return carry

            lax.fori_loop(0, CHUNKS, chunk, 0)

        @pl.when(place_ref[1] == 1)
        def _():
            ll = wide(l_ref[...].T)
            half = jnp.where(place_ref[0] == 0, ll[:H], ll[H:])

            def chunk(i, carry):
                copy(i).wait()
                def one(j, carry):
                    p = i * per + j
                    x = x_ref[pl.ds(aligned(p, D), D), :]
                    s_ref[pl.ds(p, H, stride=D), :] = product(half, stacked(x))
                    return carry

                lax.fori_loop(0, per, one, 0, unroll=min(many, per))
                return carry

            lax.fori_loop(0, CHUNKS, chunk, 0)

        done = pltpu.make_async_copy(s_ref, s_hbm, sems.at[0])
        done.start()
        done.wait()


def down_kernel(D, H, many, place_ref, x_hbm, s_hbm, e_ref, out_ref, x_ref, s_ref, n_scr, sems):
    out_ref[...] = jnp.zeros_like(out_ref)

    @pl.when(place_ref[2] == 1)
    def _():
        s_copy = fetch(s_hbm, s_ref, sems, CHUNKS)
        x_copy = fetch(x_hbm, x_ref, sems.at[pl.ds(CHUNKS, CHUNKS)], CHUNKS)
        for i in range(CHUNKS):
            s_copy(i).start()
        for i in range(CHUNKS):
            x_copy(i).start()
        start = place_ref[0] * H
        ee = wide(e_ref[...].T)
        per = 2 * H // CHUNKS

        def chunk(i, carry):
            s_copy(2 * i).wait()
            s_copy(2 * i + 1).wait()
            def one(j, carry):
                v = i * per + j
                t = s_ref[pl.ds(aligned(v, D), D), :]
                n_scr[pl.ds(v, D, stride=H), :] = product(ee, stacked(t))
                return carry

            lax.fori_loop(0, per, one, 0, unroll=min(many, per))
            return carry

        lax.fori_loop(0, CHUNKS // 2, chunk, 0)
        for i in range(CHUNKS):
            x_copy(i).wait()

        @pl.when(place_ref[1] == 0)
        def _():
            def gram(i, acc):
                q = 2 * i
                lhs = pair_rows(n_scr[pl.ds(aligned(q, H), H), :], n_scr[pl.ds(aligned(q + 1, H), H), :])
                rhs = pair_rows(x_ref[pl.ds(aligned(q, D), D), :], x_ref[pl.ds(aligned(q + 1, D), D), :])
                return acc + mm_t(lhs, rhs)

            acc = lax.fori_loop(0, D // 2, gram, jnp.zeros((2 * H, 2 * D), F32), unroll=2 * many)
            out_ref[pl.ds(aligned(place_ref[0], H), H), :] = quarters(acc)

        @pl.when(place_ref[1] == 1)
        def _():
            def gram(i, acc):
                q = 4 * i
                v = n_scr[pl.ds(aligned(i, 4 * H), 4 * H), :].T
                lhs = jnp.concatenate(split(v), 0)
                x = [x_ref[pl.ds(pl.multiple_of((q + j) * D + start, H), H), :] for j in range(4)]
                return acc + mm(lhs, wide(jnp.concatenate(x, 0)))

            acc = lax.fori_loop(0, D // 4, gram, jnp.zeros((2 * D, 2 * D), F32), unroll=many)
            out_ref[...] = quarters(acc)


def leaf_side_kernel(D, W, K, at_ref, x_hbm, xa_ref, l_ref, r_ref, t_ref, u_ref, x_ref, b_scr, sems):
    copy = fetch(x_hbm, x_ref, sems, CHUNKS)
    for i in range(CHUNKS):
        copy(i).start()
    def right(k, carry):
        rr = stacked(r_ref[k])
        for a in range(W):
            x = xa_ref[pl.ds(a, D, stride=W), :]
            t_ref[pl.ds(aligned(k * W + a, D), D), :] = product(wide(x), rr)
        return carry

    lax.fori_loop(0, K, right, 0)
    lane = lax.broadcasted_iota(jnp.int32, (W, D), 1)
    line = lax.broadcasted_iota(jnp.int32, (W, D), 0)
    pick = jnp.where(lane == line + at_ref[0] * W, 1.0, 0.0).astype(BF)
    per = D // CHUNKS

    def chunk(i, carry):
        copy(i).wait()

        def one(j, carry):
            p = i * per + j
            x = x_ref[pl.ds(aligned(p, D), D), :]
            b_scr[pl.ds(p, W, stride=D), :] = fold(mm_t(pick, jnp.concatenate(split(x), 0)))
            return carry

        return lax.fori_loop(0, per, one, carry, unroll=8)

    lax.fori_loop(0, CHUNKS, chunk, 0)

    def left(k, carry):
        ll = stacked(l_ref[k])
        for b in range(W):
            u_ref[pl.ds(aligned(k * W + b, D), D), :] = product(wide(b_scr[pl.ds(b * D, D), :]), ll)
        return carry

    lax.fori_loop(0, K, left, 0)


def leaf_kernel(D, W, K, x_hbm, t_ref, u_ref, e_ref, out_ref, x_ref, n_scr, v_scr, sems):
    copy = fetch(x_hbm, x_ref, sems, CHUNKS)
    for i in range(CHUNKS):
        copy(i).start()
    R = K * W

    def mix(k, carry):
        ee = wide(e_ref[k].T)
        for w in range(W):
            r = k * W + w
            at = pl.ds(aligned(r, D), D)
            n_scr[pl.ds(r, D, stride=R), :] = product(ee, stacked(t_ref[at, :]))
            v_scr[pl.ds(r, D, stride=R), :] = product(ee, stacked(u_ref[at, :]))
        return carry

    lax.fori_loop(0, K, mix, 0)
    def gram(i, accs):
        q = 2 * i
        one, two = pl.ds(aligned(q, R), R), pl.ds(aligned(q + 1, R), R)
        h1, l1 = split(x_ref[pl.ds(aligned(q, D), D), :])
        h2, l2 = split(x_ref[pl.ds(aligned(q + 1, D), D), :])
        cat = jnp.concatenate
        by_last = cat([cat([h1, h2], 1), cat([l1, l2], 1)], 0)
        by_first = cat([cat([h1, l1], 1), cat([h2, l2], 1)], 0)
        first = mm_t(pair_rows(n_scr[one, :], n_scr[two, :]), by_last)
        second = mm(pair_rows(v_scr[one, :], v_scr[two, :]), by_first)
        return accs[0] + first, accs[1] + second

    zero = jnp.zeros((2 * R, 2 * D), F32)
    count = D // (2 * CHUNKS)

    def chunk(i, accs):
        copy(i).wait()
        return lax.fori_loop(0, count, lambda j, a: gram(i * count + j, a), accs, unroll=4)

    first, second = lax.fori_loop(0, CHUNKS, chunk, (zero, zero))
    first = quarters(first)
    second = quarters(second)
    for k in range(K):
        out_ref[k, 0] = first[k * W : (k + 1) * W]
        out_ref[k, 1] = second[k * W : (k + 1) * W]


VMEM = pl.BlockSpec(memory_space=pltpu.VMEM)
SMEM = pl.BlockSpec(memory_space=pltpu.SMEM)
HBM = pl.BlockSpec(memory_space=pltpu.HBM)


def call(kernel, name, mib, units, out_shape, in_specs, out_specs, scratch):
    return pl.pallas_call(
        kernel,
        out_shape=out_shape,
        in_specs=in_specs,
        out_specs=out_specs,
        scratch_shapes=scratch,
        compiler_params=pltpu.CompilerParams(vmem_limit_bytes=mib << 20),
        cost_estimate=pl.CostEstimate(
            flops=int(units * 4.8e9), bytes_accessed=8 << 20, transcendentals=0
        ),
        name=name,
    )


def up_rows(place, tensor, left_env, right_env, many=16):
    D = left_env.shape[0]
    H = D // 2
    return call(
        functools.partial(up_kernel, D, H, many),
        "up",
        57,
        1,
        jax.ShapeDtypeStruct((H, D), F32),
        [SMEM, HBM, VMEM, VMEM],
        VMEM,
        [pltpu.VMEM((D * D, D), F32), pltpu.VMEM((D * H, D), F32), pltpu.SemaphoreType.DMA((2 * CHUNKS,))],
    )(place, tensor.reshape(D * D, D), left_env, right_env)


def side_part(place, tensor, left_env, right_env, many=8):
    D = left_env.shape[0]
    H = D // 2
    return call(
        functools.partial(side_kernel, D, H, many),
        "side",
        57,
        0.4,
        jax.ShapeDtypeStruct((D * H, D), F32),
        [SMEM, HBM, VMEM, VMEM],
        HBM,
        [pltpu.VMEM((D * D, D), F32), pltpu.VMEM((D * H, D), F32), pltpu.SemaphoreType.DMA((CHUNKS,))],
    )(place, tensor.reshape(D * D, D), left_env, right_env)


def down_part(place, tensor, side, above, many=16):
    D = above.shape[0]
    H = D // 2
    big = pltpu.VMEM((D * D, D), F32)
    half = pltpu.VMEM((D * H, D), F32)
    return call(
        functools.partial(down_kernel, D, H, many),
        "down",
        57,
        0.7,
        jax.ShapeDtypeStruct((D, D), F32),
        [SMEM, HBM, HBM, VMEM],
        VMEM,
        [big, half, half, pltpu.SemaphoreType.DMA((2 * CHUNKS,))],
    )(place, tensor.reshape(D * D, D), side, above)


def leaf_sides(at, whole, slab, left, right):
    K, D = left.shape[:2]
    W = slab.shape[1]
    rows = jax.ShapeDtypeStruct((K * W * D, D), F32)
    return call(
        functools.partial(leaf_side_kernel, D, W, K),
        "leaf_side",
        57,
        0.7,
        (rows, rows),
        [SMEM, HBM, VMEM, VMEM, VMEM],
        (VMEM, VMEM),
        [pltpu.VMEM((D * D, D), F32), pltpu.VMEM((W * D, D), F32), pltpu.SemaphoreType.DMA((CHUNKS,))],
    )(at.reshape(1), whole.reshape(D * D, D), slab.reshape(D * W, D), left, right)


def leaf_rows(whole, sides, above):
    K, D = above.shape[:2]
    W = sides[0].shape[0] // (K * D)
    rows = pltpu.VMEM((K * W * D, D), F32)
    return call(
        functools.partial(leaf_kernel, D, W, K),
        "leaf",
        57,
        0.7,
        jax.ShapeDtypeStruct((K, 2, W, D), F32),
        [HBM, VMEM, VMEM, VMEM],
        VMEM,
        [pltpu.VMEM((D * D, D), F32), rows, rows, pltpu.SemaphoreType.DMA((CHUNKS,))],
    )(whole.reshape(D * D, D), sides[0], sides[1], above)


NODE = ("ylo", "zhi", "zlo")
BOND = ("yhi", "x", "core")
SLOT_OF = (4, 2, 5, 1, 6, 3, 7, 0)


def ein(spec, a, b):
    return jnp.einsum(spec, a, b, precision=lax.Precision.HIGHEST)


def after(x, other):
    return lax.optimization_barrier((x, other))[0]


def other_core(x):
    return lax.ppermute(x, "core", [(0, 1), (1, 0)])


def join_cores(half, core, axis):
    other = other_core(half)
    low = jnp.where(core == 0, half, other)
    high = jnp.where(core == 0, other, half)
    return jnp.concatenate([low, high], axis=axis)


def reorder_kernel(in_ref, out_ref, sems):
    copies = [
        pltpu.make_async_copy(in_ref.at[s], out_ref.at[g], sems.at[g])
        for g, s in enumerate(SLOT_OF)
    ]
    for copy in copies:
        copy.start()
    for copy in copies:
        copy.wait()


def reordered(x):
    return pl.pallas_call(
        reorder_kernel,
        out_shape=jax.ShapeDtypeStruct(x.shape, x.dtype),
        in_specs=[HBM],
        out_specs=VMEM,
        scratch_shapes=[pltpu.SemaphoreType.DMA((len(SLOT_OF),))],
        compiler_params=pltpu.CompilerParams(vmem_limit_bytes=63 << 20),
        name="reorder",
    )(x)


def local(bottom_nodes, upper_nodes, leaf_up, outside_env, top_env):
    group = lax.axis_index(NODE)
    bond = lax.axis_index(BOND)
    core = lax.axis_index("core")
    yhi = lax.axis_index("yhi")
    op = jnp.minimum(lax.axis_index("x"), 2)
    width = bottom_nodes.shape[2]
    rows = bottom_nodes.shape[1]
    parts = width // rows

    got = lax.all_to_all(reordered(upper_nodes), NODE, 0, 0, tiled=True)
    shard = jnp.moveaxis(got, 0, 1).reshape(rows, width, width)
    upper = lax.all_gather(shard, BOND, axis=0, tiled=True)

    mine = bottom_nodes[0]
    left_leaf = leaf_up[0, :, 0]
    right_leaf = leaf_up[0, :, 1]
    middle = ein("kac,pcd->kpad", left_leaf, after(mine, shard))
    product = ein("kpad,kbd->kpab", middle, right_leaf)
    both = jnp.concatenate([mine[None], product])
    both = jnp.moveaxis(both.reshape(4, rows, parts, rows, width), 2, 0)
    both = lax.all_to_all(both, BOND, 0, 0, tiled=True)
    both = jnp.moveaxis(both, 1, 0).reshape(4, width, rows, width)
    mine_a = both[0]
    gram = ein("pab,kqab->kpq", mine_a, both[1:])
    pieces = jnp.moveaxis(gram.reshape(3, parts, rows, width), 1, 0)
    pieces = lax.all_to_all(pieces, BOND, 0, 0, tiled=True)
    env = jnp.sum(pieces, axis=0)
    by_x = jnp.stack([env[0], env[1], env[2], env[2]])
    by_dest = jnp.broadcast_to(by_x[None, None, :, None], (2, 2, 4, 2, rows, width))
    by_dest = by_dest.reshape(2 * parts, rows, width)
    pair = lax.all_to_all(by_dest, ("zlo",) + BOND, 0, 0, tiled=True)
    left3, right3 = pair.reshape(2, width, width)

    def move(x, *pairs):
        return lax.ppermute(x, NODE, pairs)

    def place(active, which=jnp.int32(0)):
        return jnp.stack([core, which, active.astype(jnp.int32)])

    is_third = group % 2 == 0
    is_second = (group == 1) | (group == 5)
    is_first = group == 3

    whole = lax.all_gather(after(mine, left3), BOND, axis=0, tiled=True)
    sides = leaf_sides(bond, whole, mine_a, left_leaf, right_leaf)

    up2 = up_rows(place(is_third), upper, left3, right3)
    ends = jnp.stack([move(up2, (0, 1), (4, 5)), move(up2, (2, 1), (6, 5))])
    left2, right2 = join_cores(ends, core, 1)
    top = lax.dynamic_index_in_dim(top_env, op, 0, keepdims=False)
    outside = lax.dynamic_index_in_dim(outside_env, op, 0, keepdims=False)
    at_crown = place(group == 7)
    crown = side_part(at_crown, upper, outside, outside, 4)
    crown = down_part(at_crown, upper, crown, top, 4)
    crown = move(crown, (7, 3))
    crown = crown + other_core(crown)
    side3 = side_part(place(is_third, yhi), upper, left3, right3, 4)
    left2, right2, side3 = lax.optimization_barrier((left2, right2, side3))
    up1 = up_rows(place(is_second), upper, left2, right2)
    ends = jnp.stack([move(up1, (1, 3)), move(up1, (5, 3))])
    left1, right1 = join_cores(ends, core, 1)
    side2 = side_part(place(is_second, yhi), upper, left2, right2, 4)
    left1, right1, side2 = lax.optimization_barrier((left1, right1, side2))

    def send_both(x, straight, across):
        axes = NODE + ("yhi",)
        return lax.ppermute(x, axes, straight), lax.ppermute(x, axes, across)

    def family(parent, one, two):
        straight = [(2 * parent, 2 * one), (2 * parent + 1, 2 * two + 1)]
        across = [(2 * parent, 2 * one + 1), (2 * parent + 1, 2 * two)]
        return straight, across

    at_first = place(is_first, yhi)
    side1 = side_part(at_first, upper, left1, right1, 16)
    made = down_part(at_first, upper, side1, crown)
    one, two = send_both(made, *family(3, 1, 5))
    above = one + two
    above = above + other_core(above)
    root = up_rows(place(is_first), upper, left1, after(right1, made), 4)
    root = join_cores(root, core, 0)
    made = down_part(place(is_second, yhi), upper, side2, above)

    fa, fb = family(1, 0, 2), family(5, 4, 6)
    one, two = send_both(
        jnp.where(is_first, root, made),
        fa[0] + fb[0] + [(6, 14), (7, 15)],
        fa[1] + fb[1] + [(6, 2), (7, 3)],
    )
    one, two, *sides = lax.optimization_barrier((one, two, *sides))
    root = jnp.where(group == 7, one, jnp.where(group == 1, two, root))
    above = one + two
    above = above + other_core(above)
    made = down_part(place(is_third, yhi), upper, side3, above)
    straight = [(1, 3), (5, 7), (9, 11), (13, 15), (0, 1), (4, 5), (8, 9), (12, 13)]
    across = [(1, 2), (5, 6), (9, 10), (13, 14)]
    straight += [(2, 0), (3, 4), (6, 8), (14, 12), (15, 10)]
    across += [(2, 1), (3, 5), (6, 9), (14, 13), (15, 11)]
    one, two = send_both(jnp.where(is_third, made, root), straight, across)
    has_root = (group == 1) | (group == 3) | (group == 7)
    root = jnp.where(has_root, root, jnp.where(yhi == 0, one, two))
    kept = jnp.where(is_third, made, two)
    last = jnp.where(yhi == 0, kept, one)
    last = last + other_core(last)
    ends = lax.all_gather(jnp.stack([last, root]), "x", axis=0, tiled=False)
    above = ends[:3, 0]
    root_env = ends[:3, 1]
    return leaf_rows(whole, sides, above)[None], root_env


def solution(mesh):
    shape = (2, 2, 2, 2, 4, 2)
    fine = Mesh(mesh.devices.reshape(shape), NODE + BOND)
    placed = (
        P(NODE, BOND, None, None),
        P(None, BOND, NODE, None),
        P(NODE, None, None, None, None),
        P(),
        P(),
    )
    return jax.shard_map(
        local,
        mesh=fine,
        in_specs=placed,
        out_specs=(P(NODE, None, None, BOND, None), P()),
        check_vma=False,
    )
```
